32 devices in a mesh: dp: 8 (over z, core), tensor: 4 (over y, x).
Axes of the slice: x: 2, y: 2, z: 4, core: 2. Of those that a mesh axis runs over, the one named last changes fastest.
Arguments:
- tokens: bfloat16 [8192, 2048], P(('dp', 'tensor')), may hold values from -6 to 6
- lengths: int32 [8, 3], P('dp'), may hold values from 1 to 512, 768 in all within a row
- query_weight: bfloat16 [2048, 2048], P('dp', 'tensor'), may hold values from -0.125 to 0.125
- key_weight: bfloat16 [2048, 2048], P('dp', 'tensor'), may hold values from -0.125 to 0.125
- value_weight: bfloat16 [2048, 2048], P('dp', 'tensor'), may hold values from -0.125 to 0.125
- output_weight: bfloat16 [2048, 2048], P('tensor', 'dp'), may hold values from -1.5 to 1.5
- gate_weight: bfloat16 [2048, 8192], P('dp', 'tensor'), may hold values from -0.125 to 0.125
- up_weight: bfloat16 [2048, 8192], P('dp', 'tensor'), may hold values from -0.125 to 0.125
- down_weight: bfloat16 [8192, 2048], P('tensor', 'dp'), may hold values from -0.0625 to 0.0625
- cotangent: bfloat16 [8192, 2048], P(('dp', 'tensor')), may hold values from -6 to 6
Outputs:
- output: bfloat16 [8192, 2048], P(('dp', 'tensor'))
- input_grad: bfloat16 [8192, 2048], P(('dp', 'tensor'))
- query_grad: float32 [2048, 2048], P('dp', 'tensor')
- key_grad: float32 [2048, 2048], P('dp', 'tensor')
- value_grad: float32 [2048, 2048], P('dp', 'tensor')
- output_grad: float32 [2048, 2048], P('tensor', 'dp')
- gate_grad: float32 [2048, 8192], P('dp', 'tensor')
- up_grad: float32 [2048, 8192], P('dp', 'tensor')
- down_grad: float32 [8192, 2048], P('tensor', 'dp')
The draws below stay inside these ranges and needn't reach their ends.
Inputs may be any that keep to these rules, and one draw needn't show every extreme that they name: Each row holds the lengths of the 3 documents packed from the start of a slot of 1024 positions; the rest of the slot is padding. Every row's largest length is 512 and its lengths add to 768.
All inputs are finite; a program needn't handle non-finite values.
Results may differ from the reference program's by a relative error of at most 0.023.
Values may be sent and summed in bfloat16 or wider, within the bound.
No kernel may reach another device: no remote copies, remote signals or barrier semaphores. Data moves between devices by JAX's collectives and lax.ppermute only.
A program may use at most 256 MiB of HBM per device.

```python
import math
import jax
import jax.numpy as jnp
import numpy as np
from jax import lax

D = 2048
H = 16
HD = 128
FF = 8192
SLOT = 1024
DOCS = 3
QBLOCK = 512
SLOTS = 8
TOKENS = 8192
N_TENSOR = 4


def block_levels(own_key, dims, split, smallest, largest):
    def one(dim, shards_of):
        steps = jax.random.uniform(jax.random.fold_in(jax.random.fold_in(own_key, 6), dim), (shards_of,), jnp.float32, smallest / len(split), largest / len(split))
        return jnp.repeat(jnp.exp(steps), dims[dim] // shards_of).reshape((-1,) + (1,) * (len(dims) - dim - 1))

    factor_of = one(*split[0])
    for cut in split[1:]:
        factor_of = factor_of * one(*cut)
    return factor_of


def profile(count, total, limit, slope):
    weights = [(1 << 20) // math.isqrt(standing ** slope) + 1 for standing in range(2, count + 1)]
    rest, given = total - limit - (count - 1), [1] * (count - 1)
    while rest > 0:
        movable = [i for i in range(count - 1) if given[i] < limit]
        mass, left = sum([weights[i] for i in movable]), rest
        for i in movable:
            addition = min(limit - given[i], max(1, left * weights[i] // mass), rest)
            given[i] = given[i] + addition
            rest = rest - addition
    return np.array([limit] + given)


def ragged_sizes(stream_key, amount, total, reach, slope):
    if amount == 2:
        one = jax.random.randint(stream_key, (), max(1, total - reach), min(reach, total - 1) + 1)
        return jnp.stack([one, total - one])
    sizes = jnp.asarray(profile(amount, total, reach, slope), jnp.int32)
    twos = (amount - 1) // 2
    source_of, receiver = sizes[1:1 + 2 * twos:2], sizes[2:2 + 2 * twos:2]
    margin = jnp.minimum(source_of - 1, reach - receiver)
    moved = jax.random.randint(jax.random.fold_in(stream_key, 1), (twos,), 0, 1 << 20) % (margin + 1)
    sizes = sizes.at[1:1 + 2 * twos:2].set(source_of - moved).at[2:2 + 2 * twos:2].set(receiver + moved)
    return sizes[jax.random.permutation(jax.random.fold_in(stream_key, 2), amount)]


def centred(rng, dims, width, most, split=(), kind=jnp.bfloat16):
    drawn = width * jax.random.normal(rng, dims, jnp.float32)
    if split:
        drawn = drawn * block_levels(rng, dims, split, -0.22, 0.18)
    return jnp.clip(drawn, -most, most).astype(kind)


def setup_inputs(seed: int = 0) -> dict:
    key_list = jax.random.split(jax.random.key(seed), 11)
    tokens = centred(key_list[0], (TOKENS, D), 1.0, 6.0, ((0, 32),))
    lengths = jax.vmap(lambda own: ragged_sizes(own, DOCS, SLOT * 3 // 4, SLOT // 2, 1))(jax.random.split(key_list[1], SLOTS)).reshape((SLOTS, DOCS)).astype(jnp.int32)
    query_weight = centred(key_list[2], (D, D), D ** -0.5, 0.125, ((0, 8), (1, 4)))
    key_weight = centred(key_list[3], (D, D), D ** -0.5, 0.125, ((0, 8), (1, 4)))
    value_weight = centred(key_list[4], (D, D), D ** -0.5, 0.125, ((0, 8), (1, 4)))
    output_weight = centred(key_list[5], (D, D), (max(D // 128, 1)) ** -0.5, 1.5, ((0, 4), (1, 8)))
    gate_weight = centred(key_list[6], (D, FF), D ** -0.5, 0.125, ((0, 8), (1, 4)))
    up_weight = centred(key_list[7], (D, FF), D ** -0.5, 0.125, ((0, 8), (1, 4)))
    down_weight = centred(key_list[8], (FF, D), FF ** -0.5, 0.0625, ((0, 4), (1, 8)))
    cotangent = centred(key_list[9], (TOKENS, D), 1.0, 6.0, ((0, 32),))
    return dict(tokens=tokens, lengths=lengths, query_weight=query_weight, key_weight=key_weight, value_weight=value_weight, output_weight=output_weight, gate_weight=gate_weight, up_weight=up_weight, down_weight=down_weight, cotangent=cotangent)


@jax.custom_vjp
def low(v):
    return lax.optimization_barrier(v.astype(jnp.bfloat16)).astype(jnp.float32)

@jax.custom_vjp
def low_back(v):
    return v

def low_keep(v):
    return (low(v), None)

def low_pass(kept, grad):
    return (grad,)

def back_keep(v):
    return (v, None)

def back_low(kept, grad):
    return (low(grad),)
low.defvjp(low_keep, low_pass)
low_back.defvjp(back_keep, back_low)
EPSILON = 1e-05
ROPE_BASE = 10000.0
MASKED = -1e+30

def layer_norm(rows):
    centre = lax.optimization_barrier(jnp.mean(rows, axis=-1, keepdims=True))
    centered = rows - centre
    spread = lax.optimization_barrier(jnp.mean(centered * centered, axis=-1, keepdims=True))
    return centered * lax.rsqrt(spread + EPSILON)

def matmul(left, right):
    return jnp.dot(left, right, precision=lax.Precision.HIGHEST, preferred_element_type=jnp.float32)

def slot_layout(lengths_row, row_total):
    ends = jnp.cumsum(lengths_row).astype(jnp.int32)
    places = jnp.arange(row_total, dtype=jnp.int32)
    segment = lax.optimization_barrier(jnp.sum((places[:, None] >= ends[None, :]).astype(jnp.int32), axis=1)).astype(jnp.int32)
    starts = jnp.concatenate([jnp.zeros((1,), jnp.int32), ends])
    picks = jnp.arange(starts.shape[0], dtype=jnp.int32)
    begins = lax.optimization_barrier(jnp.sum(jnp.where(segment[:, None] == picks[None, :], starts[None, :], 0), axis=1)).astype(jnp.int32)
    position = places - begins
    valid = (places < ends[-1]).astype(jnp.int32)
    return (segment, position, places, valid)

def rope_tables(position, head_size):
    half_size = head_size // 2
    steps_float = jnp.arange(half_size, dtype=jnp.float32)
    freqs = jnp.exp(steps_float * (-2.0 * math.log(ROPE_BASE) / head_size))
    angles = position.astype(jnp.float32)[:, None] * freqs[None, :]
    return (jnp.cos(angles), jnp.sin(angles))

def rotate(values, cosine_table, sine_table):
    half_size = values.shape[-1] // 2
    first_half = values[..., :half_size]
    second_half = values[..., half_size:]
    cosine_wide = cosine_table[:, None, :]
    sine_wide = sine_table[:, None, :]
    return jnp.concatenate([first_half * cosine_wide - second_half * sine_wide, second_half * cosine_wide + first_half * sine_wide], axis=-1)

def grouped(left, right, groups):
    row_total, inner = left.shape
    left_groups = left.reshape(row_total, groups, inner // groups)
    right_groups = right.reshape(groups, inner // groups, right.shape[1])
    partials = jnp.einsum('rgi,gio->gro', left_groups, right_groups, precision=lax.Precision.HIGHEST)
    return lax.optimization_barrier(jnp.sum(low(partials), axis=0))

def attend(queries, keys_turned, values, segment, places):
    scale = HD ** (-0.5)
    blocks = SLOT // QBLOCK
    query_blocks = queries.reshape(blocks, QBLOCK, H, HD)
    segment_blocks = segment.reshape(blocks, QBLOCK)
    place_blocks = places.reshape(blocks, QBLOCK)

    def one_block(item):
        query_block, segment_block, place_block = item
        raw_scores = jnp.einsum('qhd,khd->hqk', query_block, keys_turned, precision=lax.Precision.HIGHEST)
        scores = low_back(raw_scores) * scale
        allowed = (segment_block[:, None] == segment[None, :]) & (place_block[:, None] >= places[None, :])
        scores = jnp.where(allowed[None], scores, MASKED)
        row_peak = lax.optimization_barrier(jnp.max(scores, axis=-1, keepdims=True))
        weights = jnp.exp(scores - row_peak)
        probs = weights / lax.optimization_barrier(jnp.sum(weights, axis=-1, keepdims=True))
        return jnp.einsum('hqk,khd->qhd', low(probs), values, precision=lax.Precision.HIGHEST)
    context = lax.map(jax.checkpoint(one_block), (query_blocks, segment_blocks, place_blocks))
    return context.reshape(SLOT, H, HD)

def slot_forward(weights, inputs, lengths_row):
    query_weight, key_weight, value_weight, output_weight, gate_weight, up_weight, down_weight = weights
    segment, position, places, valid = slot_layout(lengths_row, SLOT)
    cosine_table, sine_table = rope_tables(position, HD)
    normed_one = low(layer_norm(inputs))
    query_pre = low_back(matmul(normed_one, query_weight)).reshape(SLOT, H, HD)
    key_pre = low_back(matmul(normed_one, key_weight)).reshape(SLOT, H, HD)
    values = low(low_back(matmul(normed_one, value_weight))).reshape(SLOT, H, HD)
    queries = low(rotate(query_pre, cosine_table, sine_table))
    keys_turned = low(rotate(key_pre, cosine_table, sine_table))
    context = low(low_back(attend(queries, keys_turned, values, segment, places))).reshape(SLOT, D)
    middle = inputs + low_back(grouped(context, output_weight, N_TENSOR))
    normed_two = low(layer_norm(middle))
    gate_pre = low_back(matmul(normed_two, gate_weight))
    up_pre = low_back(matmul(normed_two, up_weight))
    hidden = low(jax.nn.silu(gate_pre) * up_pre)
    feed_out = low_back(grouped(hidden, down_weight, N_TENSOR))
    return valid.astype(jnp.float32)[:, None] * (middle + feed_out)

def reference(tokens, lengths, query_weight, key_weight, value_weight, output_weight, gate_weight, up_weight, down_weight, cotangent):
    weights = tuple((matrix.astype(jnp.float32) for matrix in (query_weight, key_weight, value_weight, output_weight, gate_weight, up_weight, down_weight)))
    inputs = tokens.astype(jnp.float32).reshape(SLOTS, SLOT, D)
    step_forward = jax.checkpoint(slot_forward)

    def forward(all_inputs, all_weights):

        def step(carried, item):
            return (carried, step_forward(all_weights, item[0], item[1]))
        _, outputs = lax.scan(step, jnp.zeros((), jnp.float32), (all_inputs, lengths))
        return outputs
    outputs, pull = jax.vjp(forward, inputs, weights)
    d_inputs, d_weights = pull(cotangent.astype(jnp.float32).reshape(SLOTS, SLOT, D))
    return (outputs.reshape(TOKENS, D).astype(jnp.bfloat16), d_inputs.reshape(TOKENS, D).astype(jnp.bfloat16), d_weights[0], d_weights[1], d_weights[2], d_weights[3], d_weights[4], d_weights[5], d_weights[6])
```

```python
import math

import jax
import jax.numpy as jnp
from jax import lax
from jax.experimental import pallas as pl
from jax.experimental.pallas import tpu as pltpu
from jax.sharding import PartitionSpec as P

HD = 128
EPSILON = 1e-05
ROPE_BASE = 10000.0
MASKED = -1e30
F32 = jnp.float32
BF16 = jnp.bfloat16


def norm_forward(rows):
    centre = jnp.mean(rows, axis=-1, keepdims=True)
    centered = rows - centre
    spread = jnp.mean(centered * centered, axis=-1, keepdims=True)
    inverse = lax.rsqrt(spread + EPSILON)
    return centered * inverse, inverse


def norm_backward(normed, inverse, grad):
    mean_grad = jnp.mean(grad, axis=-1, keepdims=True)
    mean_both = jnp.mean(grad * normed, axis=-1, keepdims=True)
    return (grad - mean_grad - normed * mean_both) * inverse


def slot_layout(lengths_row, row_total):
    ends = jnp.cumsum(lengths_row)
    places = jnp.arange(row_total, dtype=jnp.int32)
    segment = jnp.sum((places[:, None] >= ends[None, :]).astype(jnp.int32), axis=1)
    starts = jnp.concatenate([jnp.zeros((1,), jnp.int32), ends])
    picks = jnp.arange(starts.shape[0], dtype=jnp.int32)
    begins = jnp.sum(jnp.where(segment[:, None] == picks[None, :], starts[None, :], 0), axis=1)
    valid = (places < ends[-1]).astype(jnp.int32)
    return segment, places - begins, valid


def rope_wide(position):
    half = HD // 2
    steps = jnp.arange(half, dtype=F32)
    freqs = jnp.exp(steps * (-2.0 * math.log(ROPE_BASE) / HD))
    angles = position.astype(F32)[:, None] * freqs[None, :]
    cosine, sine = jnp.cos(angles), jnp.sin(angles)
    return (
        jnp.concatenate([cosine, cosine], axis=1),
        jnp.concatenate([-sine, sine], axis=1),
    )


def dot_plain(left, right):
    return jnp.dot(left, right, preferred_element_type=F32)


def dot_first(left, right):
    return lax.dot_general(left, right, (((0,), (0,)), ((), ())), preferred_element_type=F32)


def dot_last(left, right):
    return lax.dot_general(left, right, (((1,), (1,)), ((), ())), preferred_element_type=F32)


def after(value, *deps):
    return lax.optimization_barrier((value,) + deps)[0]


def core_swap(value):
    count = lax.axis_size("dp")
    return lax.ppermute(value, "dp", [(k, k ^ 1) for k in range(count)])


def ring_shift(value, step):
    count = lax.axis_size("dp")
    return lax.ppermute(value, "dp", [(k, (k + 2 * step) % count) for k in range(count)])


def slot_owner(slot):
    count = lax.axis_size("dp")
    index = lax.axis_index("dp")
    chip = (index // 2 + count // 2 - slot // 2) % (count // 2)
    return chip * 2 + (index % 2 + slot % 2) % 2


def to_slots(rows):
    count = lax.axis_size("dp")
    width = rows.shape[1] // count
    return jnp.concatenate(
        [
            lax.dynamic_slice_in_dim(rows, slot_owner(slot) * width, width, 1)
            for slot in range(count)
        ],
        axis=1,
    )


def from_slots(rows):
    count = lax.axis_size("dp")
    width = rows.shape[1] // count
    index = lax.axis_index("dp")
    pieces = []
    for owner in range(count):
        lag = (index // 2 + count // 2 - owner // 2) % (count // 2)
        slot = lag * 2 + (index % 2 + owner % 2) % 2
        pieces.append(lax.dynamic_slice_in_dim(rows, slot * width, width, 1))
    return jnp.concatenate(pieces, axis=1)


def gather_slots(own, axis):
    chips = lax.axis_size("dp") // 2
    pieces = []
    for lag in range(chips):
        if lag:
            own = ring_shift(own, 1)
        pieces += [own, core_swap(own)]
    return jnp.concatenate(pieces, axis=axis), own


def scatter_slots(grad, axis):
    count = lax.axis_size("dp")
    chips = count // 2
    width = grad.shape[axis] // count

    def part(slot):
        return lax.slice_in_dim(grad, slot * width, (slot + 1) * width, axis=axis)

    def pair(lag):
        return part(2 * lag).astype(F32) + core_swap(part(2 * lag + 1)).astype(F32)

    total = pair(chips - 1).astype(BF16)
    for lag in range(chips - 2, -1, -1):
        total = ring_shift(total, -1).astype(F32) + pair(lag)
        if lag:
            total = total.astype(BF16)
    return total


def flip(value, bits):
    return lax.ppermute(value, "tensor", [(k, k ^ bits) for k in range(lax.axis_size("tensor"))])


def gather_rows(own):
    group = lax.axis_size("tensor")
    if group != 4:
        bits = 1
        while bits < group:
            own = jnp.concatenate([own, flip(own, bits)], axis=0)
            bits *= 2
        return own
    half = own.shape[0] // 2
    one = flip(own, 1)
    two = flip(own, 2)
    far_top = flip(one[:half], 2)
    far_low = flip(two[half:], 1)
    return jnp.concatenate([own, one, two, far_top, far_low], axis=0)


def scatter_rows(parts):
    group = lax.axis_size("tensor")
    if group != 4:
        while len(parts) > 1:
            bits = len(parts) // 2
            parts = [
                parts[j].astype(F32) + flip(parts[j + bits].astype(BF16), bits).astype(F32)
                for j in range(bits)
            ]
        return parts[0]
    half = parts[0].shape[0] // 2
    top = flip(parts[3][:half], 1)
    low = flip(parts[3][half:], 2)
    one_top = flip(parts[1][:half], 1)
    two_low = flip(parts[2][half:], 2)
    one_low = flip((parts[1][half:].astype(F32) + low.astype(F32)).astype(BF16), 1)
    two_top = flip((parts[2][:half].astype(F32) + top.astype(F32)).astype(BF16), 2)
    ones = jnp.concatenate([one_top, one_low], axis=0).astype(F32)
    twos = jnp.concatenate([two_top, two_low], axis=0).astype(F32)
    return parts[0].astype(F32) + ones + twos


def scores_of(q, k, seg_q, seg_k, row_base):
    s = lax.dot_general(q, k, (((1,), (1,)), ((), ())), preferred_element_type=F32) * (HD**-0.5)
    rows = lax.broadcasted_iota(jnp.int32, s.shape, 0) + row_base
    cols = lax.broadcasted_iota(jnp.int32, s.shape, 1)
    return jnp.where((seg_q == seg_k) & (rows >= cols), s, MASKED)


def softmax_of(s):
    peak = jnp.max(s, axis=-1, keepdims=True)
    e = jnp.exp(s - peak)
    return e * (1.0 / jnp.sum(e, axis=-1, keepdims=True))


def attend_kernel(blocks, t_ref, q_ref, k_ref, v_ref, segc_ref, segr_ref, out_ref, kt, vt):
    size = q_ref.shape[0] // blocks
    t = t_ref[0]

    def rows(block):
        return pl.ds(pl.multiple_of((block ^ t) * size, size), size)

    for b in range(blocks):
        kt[b * size : (b + 1) * size, :] = k_ref[rows(b), :]
        vt[b * size : (b + 1) * size, :] = v_ref[rows(b), :]
    for b in range(blocks):
        n = (b + 1) * size
        s = scores_of(
            q_ref[rows(b), :],
            kt[:n, :],
            segc_ref[b * size : n, :],
            segr_ref[:, :n],
            b * size,
        )
        p = softmax_of(s).astype(BF16)
        out_ref[rows(b), :] = jnp.dot(p, vt[:n, :], preferred_element_type=F32).astype(BF16)


def attend_forward(t, q, k, v, segc, segr):
    rows, width = q.shape
    blocks = lax.axis_size("tensor")
    head = pl.BlockSpec((rows, HD), lambda h, t: (0, h))

    def kernel(*refs):
        attend_kernel(blocks, *refs)

    return pl.pallas_call(
        kernel,
        out_shape=jax.ShapeDtypeStruct((rows, width), BF16),
        grid_spec=pltpu.PrefetchScalarGridSpec(
            num_scalar_prefetch=1,
            grid=(width // HD,),
            in_specs=[
                head,
                head,
                head,
                pl.BlockSpec((rows, 1), lambda h, t: (0, 0)),
                pl.BlockSpec((1, rows), lambda h, t: (0, 0)),
            ],
            out_specs=head,
            scratch_shapes=[pltpu.VMEM((rows, HD), BF16)] * 2,
        ),
        cost_estimate=pl.CostEstimate(
            flops=4 * rows * rows * width, bytes_accessed=8 * rows * width, transcendentals=rows * rows
        ),
    )(t, q, k, v, segc, segr)


def unattend_kernel(
    blocks, t_ref, q_ref, k_ref, v_ref, g_ref, segc_ref, segr_ref, cos_ref, sin_ref,
    dq_ref, dk_ref, dv_ref, kt, vt, dka, dva,
):
    size = q_ref.shape[0] // blocks
    t = t_ref[0]

    def rows(block):
        return pl.ds(pl.multiple_of((block ^ t) * size, size), size)

    def turn_back(grad, b):
        lo, hi = b * size, (b + 1) * size
        return grad * cos_ref[lo:hi, :] - pltpu.roll(grad, HD // 2, 1) * sin_ref[lo:hi, :]

    for b in range(blocks):
        kt[b * size : (b + 1) * size, :] = k_ref[rows(b), :]
        vt[b * size : (b + 1) * size, :] = v_ref[rows(b), :]
    for b in range(blocks - 1, -1, -1):
        n = (b + 1) * size
        q = q_ref[rows(b), :]
        g = g_ref[rows(b), :]
        s = scores_of(q, kt[:n, :], segc_ref[b * size : n, :], segr_ref[:, :n], b * size)
        p = softmax_of(s)
        dp = lax.dot_general(g, vt[:n, :], (((1,), (1,)), ((), ())), preferred_element_type=F32)
        pdp = p * dp
        delta = jnp.sum(pdp, axis=-1, keepdims=True)
        raw = ((pdp - p * delta) * (HD**-0.5)).astype(BF16)
        dq = jnp.dot(raw, kt[:n, :], preferred_element_type=F32)
        dq_ref[rows(b), :] = turn_back(dq, b).astype(BF16)
        dk = lax.dot_general(raw, q, (((0,), (0,)), ((), ())), preferred_element_type=F32)
        dv = lax.dot_general(
            p.astype(BF16), g, (((0,), (0,)), ((), ())), preferred_element_type=F32
        )
        if b == blocks - 1:
            dka[...] = dk
            dva[...] = dv
        else:
            dka[:n, :] += dk
            dva[:n, :] += dv
    for b in range(blocks):
        lo, hi = b * size, (b + 1) * size
        dk_ref[rows(b), :] = turn_back(dka[lo:hi, :], b).astype(BF16)
        dv_ref[rows(b), :] = dva[lo:hi, :].astype(BF16)


def attend_backward(t, q, k, v, g, segc, segr, cos, sin):
    rows, width = q.shape
    blocks = lax.axis_size("tensor")
    head = pl.BlockSpec((rows, HD), lambda h, t: (0, h))
    table = pl.BlockSpec((rows, HD), lambda h, t: (0, 0))

    def kernel(*refs):
        unattend_kernel(blocks, *refs)

    return pl.pallas_call(
        kernel,
        out_shape=[jax.ShapeDtypeStruct((rows, width), BF16)] * 3,
        grid_spec=pltpu.PrefetchScalarGridSpec(
            num_scalar_prefetch=1,
            grid=(width // HD,),
            in_specs=[
                head,
                head,
                head,
                head,
                pl.BlockSpec((rows, 1), lambda h, t: (0, 0)),
                pl.BlockSpec((1, rows), lambda h, t: (0, 0)),
                table,
                table,
            ],
            out_specs=[head, head, head],
            scratch_shapes=[pltpu.VMEM((rows, HD), BF16)] * 2 + [pltpu.VMEM((rows, HD), F32)] * 2,
        ),
        cost_estimate=pl.CostEstimate(
            flops=10 * rows * rows * width, bytes_accessed=14 * rows * width, transcendentals=rows * rows
        ),
    )(t, q, k, v, g, segc, segr, cos, sin)


def rotate(values, cos, sin):
    rows, width = values.shape
    heads = values.reshape(rows, width // HD, HD)
    swapped = jnp.concatenate([heads[..., HD // 2 :], heads[..., : HD // 2]], axis=-1)
    turned = heads * cos[:, None, :] + swapped * sin[:, None, :]
    return turned.reshape(rows, width).astype(BF16)


def per_device(
    tokens,
    lengths,
    query_weight,
    key_weight,
    value_weight,
    output_weight,
    gate_weight,
    up_weight,
    down_weight,
    cotangent,
):
    local = tokens.shape[0]
    group = lax.axis_size("tensor")
    t = lax.axis_index("tensor")
    slot_rows = local * group
    heads_width = query_weight.shape[1]
    hidden_width = gate_weight.shape[1]
    half_heads = heads_width // 2
    half_hidden = hidden_width // 2
    t_arg = t.astype(jnp.int32).reshape(1)

    segment, position, valid_all = slot_layout(lengths[0], slot_rows)
    valid = lax.dynamic_slice_in_dim(valid_all, t * local, local, 0).astype(F32)[:, None]
    cos, sin = rope_wide(position)
    segc, segr = segment[:, None], segment[None, :]

    def mine(table, j):
        return lax.dynamic_slice_in_dim(table, (t ^ j) * local, local, 0)

    cos_x = jnp.concatenate([mine(cos, j) for j in range(group)], axis=0)
    sin_x = jnp.concatenate([mine(sin, j) for j in range(group)], axis=0)

    heads_own = [
        jnp.concatenate(
            [w[:, a * half_heads : (a + 1) * half_heads] for w in (query_weight, key_weight, value_weight)],
            axis=1,
        )
        for a in range(2)
    ]
    gate_own = [gate_weight[:, a * half_hidden : (a + 1) * half_hidden] for a in range(2)]
    up_own = [up_weight[:, a * half_hidden : (a + 1) * half_hidden] for a in range(2)]
    down_own = [down_weight[a * half_hidden : (a + 1) * half_hidden, :] for a in range(2)]
    lanes = (
        [("a", heads_own[0], 0), ("o", output_weight, 1), ("u0", up_own[0], 0), ("g1", gate_own[1], 0), ("d1", down_own[1], 1)],
        [("b", heads_own[1], 0), ("g0", gate_own[0], 0), ("d0", down_own[0], 1), ("u1", up_own[1], 0)],
    )
    full = {}
    for lane in lanes:
        last = None
        for name, own, axis in lane:
            if last is not None:
                own = after(own, last)
            full[name], last = gather_slots(own, axis)

    residual = to_slots(tokens).astype(F32)
    grad_out = to_slots(cotangent).astype(F32) * valid
    normed_one, inverse_one = norm_forward(residual)
    h1 = gather_rows(normed_one.astype(BF16))
    g_rows = gather_rows(after(grad_out.astype(BF16), h1))

    q_parts, k_parts, v_parts, c_parts = [], [], [], []
    for name in ("a", "b"):
        pre = dot_plain(h1, full[name])
        q = rotate(pre[:, :half_heads], cos_x, sin_x)
        k = rotate(pre[:, half_heads : 2 * half_heads], cos_x, sin_x)
        v = pre[:, 2 * half_heads :].astype(BF16)
        q_parts.append(q)
        k_parts.append(k)
        v_parts.append(v)
        c_parts.append(attend_forward(t_arg, q, k, v, segc, segr))
    context = jnp.concatenate(c_parts, axis=1)

    def row_piece(value, j):
        return value[j * local : (j + 1) * local]

    attention = scatter_rows(
        [dot_plain(row_piece(context, j), full["o"]).astype(BF16) for j in range(group)]
    )
    middle = residual + attention
    normed_two, inverse_two = norm_forward(middle)
    h2 = gather_rows(normed_two.astype(BF16))

    feed = [None] * group
    d_normed = [None] * group
    sums = {}
    for a in range(2):
        gate_w, up_w, down_w = full[f"g{a}"], full[f"u{a}"], full[f"d{a}"]
        d_hidden = dot_last(g_rows, down_w)
        gate = dot_plain(h2, gate_w)
        up = dot_plain(h2, up_w)
        sg = jax.nn.sigmoid(gate)
        act = gate * sg
        hidden = (act * up).astype(BF16)
        d_gate = (d_hidden * up * sg * (1.0 + gate * (1.0 - sg))).astype(BF16)
        d_up = (d_hidden * act).astype(BF16)
        sums[f"d{a}"] = scatter_slots(dot_first(hidden, g_rows).astype(BF16), 1)
        sums[f"g{a}"] = scatter_slots(dot_first(h2, d_gate).astype(BF16), 0)
        sums[f"u{a}"] = scatter_slots(dot_first(h2, d_up).astype(BF16), 0)
        for j in range(group):
            f = dot_plain(row_piece(hidden, j), down_w)
            d = dot_last(row_piece(d_gate, j), gate_w) + dot_last(row_piece(d_up, j), up_w)
            feed[j] = f if a == 0 else feed[j] + f
            d_normed[j] = d if a == 0 else d_normed[j] + d
    d_normed_two = scatter_rows([d.astype(BF16) for d in d_normed])
    d_middle = grad_out + norm_backward(normed_two, inverse_two, d_normed_two)
    d_attention = gather_rows(d_middle.astype(BF16))

    feed_out = scatter_rows([f.astype(BF16) for f in feed])
    output = from_slots((valid * (middle + feed_out)).astype(BF16))

    d_context = dot_last(d_attention, full["o"]).astype(BF16)
    sums["o"] = scatter_slots(dot_first(context, d_attention).astype(BF16), 1)
    d_one = [None] * group
    for a, name in enumerate(("a", "b")):
        d_q, d_k, d_v = attend_backward(
            t_arg,
            q_parts[a],
            k_parts[a],
            v_parts[a],
            d_context[:, a * half_heads : (a + 1) * half_heads],
            segc,
            segr,
            cos,
            sin,
        )
        d_pre = jnp.concatenate([d_q, d_k, d_v], axis=1)
        sums[name] = scatter_slots(dot_first(h1, d_pre).astype(BF16), 0)
        for j in range(group):
            d = dot_last(row_piece(d_pre, j), full[name])
            d_one[j] = d if a == 0 else d_one[j] + d
    d_normed_one = scatter_rows([d.astype(BF16) for d in d_one])
    input_grad = from_slots(
        (d_middle + norm_backward(normed_one, inverse_one, d_normed_one)).astype(BF16)
    )

    def heads_grad(which):
        lo, hi = which * half_heads, (which + 1) * half_heads
        return jnp.concatenate([sums["a"][:, lo:hi], sums["b"][:, lo:hi]], axis=1)

    return (
        output,
        input_grad,
        heads_grad(0),
        heads_grad(1),
        heads_grad(2),
        sums["o"],
        jnp.concatenate([sums["g0"], sums["g1"]], axis=1),
        jnp.concatenate([sums["u0"], sums["u1"]], axis=1),
        jnp.concatenate([sums["d0"], sums["d1"]], axis=0),
    )


def solution(mesh):
    return jax.shard_map(
        per_device,
        mesh=mesh,
        in_specs=(
            P(("dp", "tensor"), None),
            P("dp", None),
            P("dp", "tensor"),
            P("dp", "tensor"),
            P("dp", "tensor"),
            P("tensor", "dp"),
            P("dp", "tensor"),
            P("dp", "tensor"),
            P("tensor", "dp"),
            P(("dp", "tensor"), None),
        ),
        out_specs=(
            P(("dp", "tensor"), None),
            P(("dp", "tensor"), None),
            P("dp", "tensor"),
            P("dp", "tensor"),
            P("dp", "tensor"),
            P("tensor", "dp"),
            P("dp", "tensor"),
            P("dp", "tensor"),
            P("tensor", "dp"),
        ),
        check_vma=False,
    )
```

```python
import math

import jax
import jax.numpy as jnp
from jax import lax
from jax.experimental import pallas as pl
from jax.experimental.pallas import tpu as pltpu
from jax.sharding import PartitionSpec as P

HD = 128
EPSILON = 1e-05
ROPE_BASE = 10000.0
MASKED = -1e30
F32 = jnp.float32
BF16 = jnp.bfloat16


def norm_forward(rows):
    centre = jnp.mean(rows, axis=-1, keepdims=True)
    centered = rows - centre
    spread = jnp.mean(centered * centered, axis=-1, keepdims=True)
    inverse = lax.rsqrt(spread + EPSILON)
    return centered * inverse, inverse


def norm_backward(normed, inverse, grad):
    mean_grad = jnp.mean(grad, axis=-1, keepdims=True)
    mean_both = jnp.mean(grad * normed, axis=-1, keepdims=True)
    return (grad - mean_grad - normed * mean_both) * inverse


def slot_layout(lengths_row, row_total):
    ends = jnp.cumsum(lengths_row)
    places = jnp.arange(row_total, dtype=jnp.int32)
    segment = jnp.sum((places[:, None] >= ends[None, :]).astype(jnp.int32), axis=1)
    starts = jnp.concatenate([jnp.zeros((1,), jnp.int32), ends])
    picks = jnp.arange(starts.shape[0], dtype=jnp.int32)
    begins = jnp.sum(jnp.where(segment[:, None] == picks[None, :], starts[None, :], 0), axis=1)
    valid = (places < ends[-1]).astype(jnp.int32)
    return segment, places - begins, valid


def rope_wide(position):
    half = HD // 2
    steps = jnp.arange(half, dtype=F32)
    freqs = jnp.exp(steps * (-2.0 * math.log(ROPE_BASE) / HD))
    angles = position.astype(F32)[:, None] * freqs[None, :]
    cosine, sine = jnp.cos(angles), jnp.sin(angles)
    return (
        jnp.concatenate([cosine, cosine], axis=1),
        jnp.concatenate([-sine, sine], axis=1),
    )


def dot_plain(left, right):
    return jnp.dot(left, right, preferred_element_type=F32)


def dot_first(left, right):
    return lax.dot_general(left, right, (((0,), (0,)), ((), ())), preferred_element_type=F32)


def dot_last(left, right):
    return lax.dot_general(left, right, (((1,), (1,)), ((), ())), preferred_element_type=F32)


def after(value, *deps):
    return lax.optimization_barrier((value,) + deps)[0]


def gather_dp(own, axis):
    return lax.all_gather(own, "dp", axis=axis, tiled=True)


def scatter_dp(grad, axis):
    total = lax.psum_scatter(grad.astype(BF16), "dp", scatter_dimension=axis, tiled=True)
    return total.astype(F32)


def flip(value, bits):
    return lax.ppermute(value, "tensor", [(k, k ^ bits) for k in range(lax.axis_size("tensor"))])


def join_kernel(*refs):
    out = refs[-1]
    start = 0
    for ref in refs[:-1]:
        out[start : start + ref.shape[0], :] = ref[...]
        start += ref.shape[0]


def join(pieces):
    rows = sum(piece.shape[0] for piece in pieces)
    width = pieces[0].shape[1]
    tile = min(width, 512)
    return pl.pallas_call(
        join_kernel,
        out_shape=jax.ShapeDtypeStruct((rows, width), pieces[0].dtype),
        grid=(width // tile,),
        in_specs=[pl.BlockSpec((piece.shape[0], tile), lambda n: (0, n)) for piece in pieces],
        out_specs=pl.BlockSpec((rows, tile), lambda n: (0, n)),
        cost_estimate=pl.CostEstimate(flops=0, bytes_accessed=4 * rows * width, transcendentals=0),
    )(*pieces)


def gather_rows(own):
    return gather_steps(own)[0]


def gather_steps(own):
    group = lax.axis_size("tensor")
    if group != 4:
        bits = 1
        while bits < group:
            own = jnp.concatenate([own, flip(own, bits)], axis=0)
            bits *= 2
        return own, own
    half = own.shape[0] // 2
    one = flip(own, 1)
    two = flip(own, 2)
    far_top = flip(one[:half], 2)
    far_low = flip(two[half:], 1)
    return join([own, one, two, far_top, far_low]), one


def scatter_rows(piece):
    group = lax.axis_size("tensor")
    if group != 4:
        parts = [piece(j, None).astype(BF16) for j in range(group)]
        while len(parts) > 1:
            bits = len(parts) // 2
            parts = [
                parts[j].astype(F32) + flip(parts[j + bits].astype(BF16), bits).astype(F32)
                for j in range(bits)
            ]
        return parts[0]
    far = piece(3, None).astype(BF16)
    half = far.shape[0] // 2
    top = flip(far[:half], 1)
    low = flip(far[half:], 2)
    one = piece(1, far).astype(BF16)
    one_top = flip(one[:half], 1)
    two = piece(2, one).astype(BF16)
    two_low = flip(two[half:], 2)
    one_low = flip((one[half:].astype(F32) + low.astype(F32)).astype(BF16), 1)
    two_top = flip((two[:half].astype(F32) + top.astype(F32)).astype(BF16), 2)
    own = piece(0, two)
    ones = jnp.concatenate([one_top, one_low], axis=0).astype(F32)
    twos = jnp.concatenate([two_top, two_low], axis=0).astype(F32)
    return own + ones + twos


def feed_kernel(h_ref, g_ref, gate_ref, up_ref, down_ref, hidden_ref, d_ref):
    tile = gate_ref.shape[1]
    lo = pl.program_id(0) * tile
    gate = jnp.dot(h_ref[...], gate_ref[...], preferred_element_type=F32)
    up = jnp.dot(h_ref[...], up_ref[...], preferred_element_type=F32)
    d_hidden = jnp.dot(g_ref[...], down_ref[...], preferred_element_type=F32)
    sg = jax.nn.sigmoid(gate)
    act = gate * sg
    hidden_ref[...] = (act * up).astype(BF16)
    d_gate = d_hidden * up * (sg + act * (1.0 - sg))
    d_ref[:, pl.ds(pl.multiple_of(lo, tile), tile)] = d_gate.astype(BF16)
    d_ref[:, pl.ds(pl.multiple_of(lo + d_ref.shape[1] // 2, tile), tile)] = (d_hidden * act).astype(BF16)


def feed(h2, g_rows, wide):
    rows, depth = h2.shape
    width = wide.shape[1] // 3
    tile = 256
    tiles = width // tile
    return pl.pallas_call(
        feed_kernel,
        out_shape=[
            jax.ShapeDtypeStruct((rows, width), BF16),
            jax.ShapeDtypeStruct((rows, 2 * width), BF16),
        ],
        grid=(tiles,),
        in_specs=[
            pl.BlockSpec((rows, depth), lambda n: (0, 0)),
            pl.BlockSpec((rows, depth), lambda n: (0, 0)),
            pl.BlockSpec((depth, tile), lambda n: (0, n)),
            pl.BlockSpec((depth, tile), lambda n: (0, tiles + n)),
            pl.BlockSpec((depth, tile), lambda n: (0, 2 * tiles + n)),
        ],
        out_specs=[
            pl.BlockSpec((rows, tile), lambda n: (0, n)),
            pl.BlockSpec((rows, 2 * width), lambda n: (0, 0)),
        ],
        cost_estimate=pl.CostEstimate(
            flops=6 * rows * depth * width,
            bytes_accessed=4 * rows * depth + 6 * depth * width + 6 * rows * width,
            transcendentals=rows * width,
        ),
    )(h2, g_rows, wide, wide, wide)


def scores_of(q, k, seg_q, seg_k, row_base):
    s = lax.dot_general(q, k, (((1,), (1,)), ((), ())), preferred_element_type=F32) * (HD**-0.5)
    rows = lax.broadcasted_iota(jnp.int32, s.shape, 0) + row_base
    cols = lax.broadcasted_iota(jnp.int32, s.shape, 1)
    return jnp.where((seg_q == seg_k) & (rows >= cols), s, MASKED)


def softmax_of(s):
    peak = jnp.max(s, axis=-1, keepdims=True)
    e = jnp.exp(s - peak)
    return e * (1.0 / jnp.sum(e, axis=-1, keepdims=True))


def turn(values, cos, sin):
    return values * cos + pltpu.roll(values, HD // 2, 1) * sin


def attend_kernel(
    blocks, t_ref, q_ref, k_ref, v_ref, segc_ref, segr_ref, cos_ref, sin_ref,
    out_ref, saved_ref, kt, vt,
):
    size = q_ref.shape[0] // blocks
    width = saved_ref.shape[1] // 3
    head = pl.program_id(0) * HD
    t = t_ref[0]

    def rows(block):
        return pl.ds(pl.multiple_of((block ^ t) * size, size), size)

    def lanes(which):
        return pl.ds(pl.multiple_of(which * width + head, HD), HD)

    for b in range(blocks):
        lo, hi = b * size, (b + 1) * size
        cos, sin = cos_ref[lo:hi, :], sin_ref[lo:hi, :]
        q = turn(q_ref[rows(b), :], cos, sin).astype(BF16)
        k = turn(k_ref[rows(b), :], cos, sin).astype(BF16)
        v = v_ref[rows(b), :].astype(BF16)
        saved_ref[rows(b), lanes(0)] = q
        saved_ref[rows(b), lanes(1)] = k
        saved_ref[rows(b), lanes(2)] = v
        kt[lo:hi, :] = k
        vt[lo:hi, :] = v
        s = scores_of(q, kt[:hi, :], segc_ref[lo:hi, :], segr_ref[:, :hi], lo)
        p = softmax_of(s).astype(BF16)
        out_ref[rows(b), :] = jnp.dot(p, vt[:hi, :], preferred_element_type=F32).astype(BF16)


def attend_forward(t, pre, segc, segr, cos, sin):
    rows, width = pre.shape[0], pre.shape[1] // 3
    heads = width // HD
    blocks = lax.axis_size("tensor")
    table = pl.BlockSpec((rows, HD), lambda h, t: (0, 0))

    def kernel(*refs):
        attend_kernel(blocks, *refs)

    return pl.pallas_call(
        kernel,
        out_shape=[
            jax.ShapeDtypeStruct((rows, width), BF16),
            jax.ShapeDtypeStruct((rows, 3 * width), BF16),
        ],
        grid_spec=pltpu.PrefetchScalarGridSpec(
            num_scalar_prefetch=1,
            grid=(heads,),
            in_specs=[
                pl.BlockSpec((rows, HD), lambda h, t: (0, h)),
                pl.BlockSpec((rows, HD), lambda h, t: (0, heads + h)),
                pl.BlockSpec((rows, HD), lambda h, t: (0, 2 * heads + h)),
                pl.BlockSpec((rows, 1), lambda h, t: (0, 0)),
                pl.BlockSpec((1, rows), lambda h, t: (0, 0)),
                table,
                table,
            ],
            out_specs=[
                pl.BlockSpec((rows, HD), lambda h, t: (0, h)),
                pl.BlockSpec((rows, 3 * width), lambda h, t: (0, 0)),
            ],
            scratch_shapes=[pltpu.VMEM((rows, HD), BF16)] * 2,
        ),
        cost_estimate=pl.CostEstimate(
            flops=4 * rows * rows * width,
            bytes_accessed=20 * rows * width,
            transcendentals=rows * rows * heads,
        ),
    )(t, pre, pre, pre, segc, segr, cos, sin)


def unattend_kernel(
    blocks, t_ref, q_ref, k_ref, v_ref, g_ref, segc_ref, segr_ref, cos_ref, sin_ref,
    out_ref, kt, vt, dka, dva,
):
    size = q_ref.shape[0] // blocks
    width = out_ref.shape[1] // 3
    head = pl.program_id(0) * HD
    t = t_ref[0]

    def rows(block):
        return pl.ds(pl.multiple_of((block ^ t) * size, size), size)

    def lanes(which):
        return pl.ds(pl.multiple_of(which * width + head, HD), HD)

    def turn_back(grad, b):
        lo, hi = b * size, (b + 1) * size
        return grad * cos_ref[lo:hi, :] - pltpu.roll(grad, HD // 2, 1) * sin_ref[lo:hi, :]

    for b in range(blocks):
        kt[b * size : (b + 1) * size, :] = k_ref[rows(b), :]
        vt[b * size : (b + 1) * size, :] = v_ref[rows(b), :]
    for b in range(blocks - 1, -1, -1):
        n = (b + 1) * size
        q = q_ref[rows(b), :]
        g = g_ref[rows(b), :]
        s = scores_of(q, kt[:n, :], segc_ref[b * size : n, :], segr_ref[:, :n], b * size)
        p = softmax_of(s)
        dp = lax.dot_general(g, vt[:n, :], (((1,), (1,)), ((), ())), preferred_element_type=F32)
        pdp = p * dp
        delta = jnp.sum(pdp, axis=-1, keepdims=True)
        raw = ((pdp - p * delta) * (HD**-0.5)).astype(BF16)
        dq = jnp.dot(raw, kt[:n, :], preferred_element_type=F32)
        out_ref[rows(b), lanes(0)] = turn_back(dq, b).astype(BF16)
        dk = lax.dot_general(raw, q, (((0,), (0,)), ((), ())), preferred_element_type=F32)
        dv = lax.dot_general(
            p.astype(BF16), g, (((0,), (0,)), ((), ())), preferred_element_type=F32
        )
        if b == blocks - 1:
            dka[...] = dk
            dva[...] = dv
        else:
            dka[:n, :] += dk
            dva[:n, :] += dv
    for b in range(blocks):
        lo, hi = b * size, (b + 1) * size
        out_ref[rows(b), lanes(1)] = turn_back(dka[lo:hi, :], b).astype(BF16)
        out_ref[rows(b), lanes(2)] = dva[lo:hi, :].astype(BF16)


def attend_backward(t, saved, g, segc, segr, cos, sin):
    rows, width = g.shape
    heads = width // HD
    blocks = lax.axis_size("tensor")
    table = pl.BlockSpec((rows, HD), lambda h, t: (0, 0))

    def kernel(*refs):
        unattend_kernel(blocks, *refs)

    return pl.pallas_call(
        kernel,
        out_shape=jax.ShapeDtypeStruct((rows, 3 * width), BF16),
        grid_spec=pltpu.PrefetchScalarGridSpec(
            num_scalar_prefetch=1,
            grid=(heads,),
            in_specs=[
                pl.BlockSpec((rows, HD), lambda h, t: (0, h)),
                pl.BlockSpec((rows, HD), lambda h, t: (0, heads + h)),
                pl.BlockSpec((rows, HD), lambda h, t: (0, 2 * heads + h)),
                pl.BlockSpec((rows, HD), lambda h, t: (0, h)),
                pl.BlockSpec((rows, 1), lambda h, t: (0, 0)),
                pl.BlockSpec((1, rows), lambda h, t: (0, 0)),
                table,
                table,
            ],
            out_specs=pl.BlockSpec((rows, 3 * width), lambda h, t: (0, 0)),
            scratch_shapes=[pltpu.VMEM((rows, HD), BF16)] * 2 + [pltpu.VMEM((rows, HD), F32)] * 2,
        ),
        cost_estimate=pl.CostEstimate(
            flops=10 * rows * rows * width,
            bytes_accessed=14 * rows * width,
            transcendentals=rows * rows * heads,
        ),
    )(t, saved, saved, saved, g, segc, segr, cos, sin)


def per_device(
    tokens,
    lengths,
    query_weight,
    key_weight,
    value_weight,
    output_weight,
    gate_weight,
    up_weight,
    down_weight,
    cotangent,
):
    local = tokens.shape[0]
    group = lax.axis_size("tensor")
    t = lax.axis_index("tensor")
    slot_rows = local * group
    heads_width = query_weight.shape[1]
    hidden_width = gate_weight.shape[1]
    t_arg = t.astype(jnp.int32).reshape(1)

    half = hidden_width // 2

    mixed = gather_dp(
        jnp.concatenate([query_weight, key_weight, value_weight, output_weight.T], axis=1), 0
    )
    heads_full, out_full = mixed[:, : 3 * heads_width], mixed[:, 3 * heads_width :]
    wide = [
        gather_dp(
            jnp.concatenate(
                [w[:, a * half : (a + 1) * half] for w in (gate_weight, up_weight)]
                + [down_weight[a * half : (a + 1) * half].T],
                axis=1,
            ),
            0,
        )
        for a in range(2)
    ]

    segment, position, valid_all = slot_layout(lengths[0], slot_rows)
    valid = lax.dynamic_slice_in_dim(valid_all, t * local, local, 0).astype(F32)[:, None]
    cos, sin = rope_wide(position)
    segc, segr = segment[:, None], segment[None, :]

    residual = tokens.astype(F32)
    grad_out = cotangent.astype(F32) * valid
    normed_one, inverse_one = norm_forward(residual)
    h1 = gather_rows(normed_one.astype(BF16))
    g_rows = gather_rows(after(grad_out.astype(BF16), h1))

    def rows_of(value, j):
        return value[j * local : (j + 1) * local]

    context, saved = attend_forward(t_arg, dot_plain(h1, heads_full), segc, segr, cos, sin)

    def attention_piece(j, earlier):
        rows = rows_of(context, j)
        return dot_last(rows if earlier is None else after(rows, earlier), out_full)

    middle = residual + scatter_rows(attention_piece)
    normed_two, inverse_two = norm_forward(middle)
    h2 = gather_rows(normed_two.astype(BF16))

    hidden_0, d_wide_0 = feed(h2, g_rows, wide[0])
    first_grad = jnp.concatenate(
        [dot_first(h2, d_wide_0).astype(BF16), dot_first(g_rows, hidden_0).astype(BF16)], axis=1
    )
    first_sum = scatter_dp(first_grad, 0)
    d_first = dot_last(d_wide_0, wide[0][:, : 2 * half])
    wide_1, first_grad, d_first = lax.optimization_barrier((wide[1], first_grad, d_first))
    hidden_1, d_wide_1 = feed(h2, g_rows, wide_1)

    def feed_back_piece(j, earlier):
        rows = rows_of(d_wide_1, j)
        rows = rows if earlier is None else after(rows, earlier)
        return rows_of(d_first, j) + dot_last(rows, wide_1[:, : 2 * half])

    d_normed_two = scatter_rows(feed_back_piece)
    d_middle = grad_out + norm_backward(normed_two, inverse_two, d_normed_two)
    second_grad = jnp.concatenate(
        [dot_first(h2, d_wide_1).astype(BF16), dot_first(g_rows, hidden_1).astype(BF16)], axis=1
    )
    d_attention = gather_rows(d_middle.astype(BF16))
    d_context = dot_plain(d_attention, out_full).astype(BF16)
    second_sum = scatter_dp(after(second_grad, first_sum, d_context), 0)

    def feed_piece(j, earlier):
        rows = after(rows_of(hidden_0, j), d_attention if earlier is None else earlier)
        return dot_last(rows, wide[0][:, 2 * half :]) + dot_last(
            rows_of(hidden_1, j), wide_1[:, 2 * half :]
        )

    feed_out = scatter_rows(feed_piece)

    d_pre = attend_backward(t_arg, saved, d_context, segc, segr, cos, sin)
    d_pre = after(d_pre, feed_out)
    output = (valid * (middle + feed_out)).astype(BF16)
    mixed_grad = jnp.concatenate(
        [dot_first(h1, d_pre).astype(BF16), dot_first(d_attention, context).astype(BF16)], axis=1
    )
    mixed_sum = scatter_dp(after(mixed_grad, second_sum), 0)

    def heads_back_piece(j, earlier):
        rows = rows_of(d_pre, j)
        return dot_last(rows if earlier is None else after(rows, earlier), heads_full)

    d_normed_one = scatter_rows(heads_back_piece)
    input_grad = (d_middle + norm_backward(normed_one, inverse_one, d_normed_one)).astype(BF16)
    wide_sum = [first_sum, second_sum]

    return (
        output,
        input_grad,
        mixed_sum[:, :heads_width],
        mixed_sum[:, heads_width : 2 * heads_width],
        mixed_sum[:, 2 * heads_width : 3 * heads_width],
        mixed_sum[:, 3 * heads_width :].T,
        jnp.concatenate([part[:, :half] for part in wide_sum], axis=1),
        jnp.concatenate([part[:, half : 2 * half] for part in wide_sum], axis=1),
        jnp.concatenate([part[:, 2 * half :].T for part in wide_sum], axis=0),
    )


def solution(mesh):
    return jax.shard_map(
        per_device,
        mesh=mesh,
        in_specs=(
            P(("dp", "tensor"), None),
            P("dp", None),
            P("dp", "tensor"),
            P("dp", "tensor"),
            P("dp", "tensor"),
            P("tensor", "dp"),
            P("dp", "tensor"),
            P("dp", "tensor"),
            P("tensor", "dp"),
            P(("dp", "tensor"), None),
        ),
        out_specs=(
            P(("dp", "tensor"), None),
            P(("dp", "tensor"), None),
            P("dp", "tensor"),
            P("dp", "tensor"),
            P("dp", "tensor"),
            P("tensor", "dp"),
            P("dp", "tensor"),
            P("dp", "tensor"),
            P("tensor", "dp"),
        ),
        check_vma=False,
    )
```

```python
import math

import jax
import jax.numpy as jnp
from jax import lax
from jax.experimental import pallas as pl
from jax.experimental.pallas import tpu as pltpu
from jax.sharding import PartitionSpec as P

HD = 128
EPSILON = 1e-05
ROPE_BASE = 10000.0
MASKED = -1e30
F32 = jnp.float32
BF16 = jnp.bfloat16


def norm_forward(rows):
    centre = jnp.mean(rows, axis=-1, keepdims=True)
    centered = rows - centre
    spread = jnp.mean(centered * centered, axis=-1, keepdims=True)
    inverse = lax.rsqrt(spread + EPSILON)
    return centered * inverse, inverse


def norm_backward(normed, inverse, grad):
    mean_grad = jnp.mean(grad, axis=-1, keepdims=True)
    mean_both = jnp.mean(grad * normed, axis=-1, keepdims=True)
    return (grad - mean_grad - normed * mean_both) * inverse


def slot_layout(lengths_row, row_total):
    ends = jnp.cumsum(lengths_row)
    places = jnp.arange(row_total, dtype=jnp.int32)
    segment = jnp.sum((places[:, None] >= ends[None, :]).astype(jnp.int32), axis=1)
    starts = jnp.concatenate([jnp.zeros((1,), jnp.int32), ends])
    picks = jnp.arange(starts.shape[0], dtype=jnp.int32)
    begins = jnp.sum(jnp.where(segment[:, None] == picks[None, :], starts[None, :], 0), axis=1)
    valid = (places < ends[-1]).astype(jnp.int32)
    return segment, places - begins, valid


def rope_wide(position):
    half = HD // 2
    steps = jnp.arange(half, dtype=F32)
    freqs = jnp.exp(steps * (-2.0 * math.log(ROPE_BASE) / HD))
    angles = position.astype(F32)[:, None] * freqs[None, :]
    cosine, sine = jnp.cos(angles), jnp.sin(angles)
    return (
        jnp.concatenate([cosine, cosine], axis=1),
        jnp.concatenate([-sine, sine], axis=1),
    )


def dot_plain(left, right):
    return jnp.dot(left, right, preferred_element_type=F32)


def dot_first(left, right):
    return lax.dot_general(left, right, (((0,), (0,)), ((), ())), preferred_element_type=F32)


def dot_last(left, right):
    return lax.dot_general(left, right, (((1,), (1,)), ((), ())), preferred_element_type=F32)


def after(value, *deps):
    return lax.optimization_barrier((value,) + deps)[0]


def gather_dp(own, axis):
    return lax.all_gather(own, "dp", axis=axis, tiled=True)


def core_swap(value):
    count = lax.axis_size("dp")
    return lax.ppermute(value, "dp", [(k, k ^ 1) for k in range(count)])


def pair_sum(terms):
    others = [core_swap(dot_first(peer, right).astype(BF16)) for own, peer, right in terms]
    sums = [
        (dot_first(own, right) + other.astype(F32)).astype(BF16)
        for (own, peer, right), other in zip(terms, others)
    ]
    return jnp.concatenate(sums, axis=1)


def scatter_dp(pairs):
    count = lax.axis_size("dp")
    groups = [list(range(core, count, 2)) for core in range(2)]
    total = lax.psum_scatter(
        pairs, "dp", scatter_dimension=0, tiled=True, axis_index_groups=groups
    )
    return total.astype(F32)


def flip(value, bits):
    return lax.ppermute(value, "tensor", [(k, k ^ bits) for k in range(lax.axis_size("tensor"))])


def join_kernel(core_ref, *refs):
    out, own, peer = refs[-3:]
    width = own.shape[1]
    mine = pl.multiple_of(core_ref[0] * width, width)
    other = pl.multiple_of((1 - core_ref[0]) * width, width)
    start = 0
    for ref in refs[:-3]:
        rows = slice(start, start + ref.shape[0])
        out[rows, :] = ref[...]
        own[rows, :] = ref[:, pl.ds(mine, width)]
        peer[rows, :] = ref[:, pl.ds(other, width)]
        start += ref.shape[0]


def join(pieces):
    rows = sum(piece.shape[0] for piece in pieces)
    width = pieces[0].shape[1]
    count = lax.axis_size("dp")
    tile = 2 * width // count
    core = (lax.axis_index("dp") % 2).astype(jnp.int32).reshape(1)
    half = pl.BlockSpec((rows, tile // 2), lambda n, c: (0, n))
    return pl.pallas_call(
        join_kernel,
        out_shape=[
            jax.ShapeDtypeStruct((rows, width), pieces[0].dtype),
            jax.ShapeDtypeStruct((rows, width // 2), pieces[0].dtype),
            jax.ShapeDtypeStruct((rows, width // 2), pieces[0].dtype),
        ],
        grid_spec=pltpu.PrefetchScalarGridSpec(
            num_scalar_prefetch=1,
            grid=(count // 2,),
            in_specs=[pl.BlockSpec((piece.shape[0], tile), lambda n, c: (0, n)) for piece in pieces],
            out_specs=[pl.BlockSpec((rows, tile), lambda n, c: (0, n)), half, half],
        ),
        cost_estimate=pl.CostEstimate(flops=0, bytes_accessed=6 * rows * width, transcendentals=0),
    )(core, *pieces)


def gather_rows(own):
    return gather_steps(own)[0]


def gather_steps(own):
    group = lax.axis_size("tensor")
    if group != 4:
        bits = 1
        while bits < group:
            own = jnp.concatenate([own, flip(own, bits)], axis=0)
            bits *= 2
        return join([own]), own
    half = own.shape[0] // 2
    one = flip(own, 1)
    two = flip(own, 2)
    far_top = flip(one[:half], 2)
    far_low = flip(two[half:], 1)
    return join([own, one, two, far_top, far_low]), one


def scatter_rows(piece):
    group = lax.axis_size("tensor")
    if group != 4:
        parts = [piece(j, None).astype(BF16) for j in range(group)]
        while len(parts) > 1:
            bits = len(parts) // 2
            parts = [
                parts[j].astype(F32) + flip(parts[j + bits].astype(BF16), bits).astype(F32)
                for j in range(bits)
            ]
        return parts[0]
    far = piece(3, None).astype(BF16)
    half = far.shape[0] // 2
    top = flip(far[:half], 1)
    low = flip(far[half:], 2)
    one = piece(1, far).astype(BF16)
    one_top = flip(one[:half], 1)
    two = piece(2, one).astype(BF16)
    two_low = flip(two[half:], 2)
    one_low = flip((one[half:].astype(F32) + low.astype(F32)).astype(BF16), 1)
    two_top = flip((two[:half].astype(F32) + top.astype(F32)).astype(BF16), 2)
    own = piece(0, two)
    ones = jnp.concatenate([one_top, one_low], axis=0).astype(F32)
    twos = jnp.concatenate([two_top, two_low], axis=0).astype(F32)
    return own + ones + twos


def feed_kernel(h_ref, g_ref, gate_ref, up_ref, down_ref, hidden_ref, d_ref):
    tile = gate_ref.shape[1]
    lo = pl.program_id(0) * tile
    gate = jnp.dot(h_ref[...], gate_ref[...], preferred_element_type=F32)
    up = jnp.dot(h_ref[...], up_ref[...], preferred_element_type=F32)
    d_hidden = jnp.dot(g_ref[...], down_ref[...], preferred_element_type=F32)
    sg = jax.nn.sigmoid(gate)
    act = gate * sg
    hidden_ref[...] = (act * up).astype(BF16)
    d_gate = d_hidden * up * (sg + act * (1.0 - sg))
    d_ref[:, pl.ds(pl.multiple_of(lo, tile), tile)] = d_gate.astype(BF16)
    d_ref[:, pl.ds(pl.multiple_of(lo + d_ref.shape[1] // 2, tile), tile)] = (d_hidden * act).astype(BF16)


def feed(h2, g_rows, wide):
    rows, depth = h2.shape
    width = wide.shape[1] // 3
    tile = 256
    tiles = width // tile
    return pl.pallas_call(
        feed_kernel,
        out_shape=[
            jax.ShapeDtypeStruct((rows, width), BF16),
            jax.ShapeDtypeStruct((rows, 2 * width), BF16),
        ],
        grid=(tiles,),
        in_specs=[
            pl.BlockSpec((rows, depth), lambda n: (0, 0)),
            pl.BlockSpec((rows, depth), lambda n: (0, 0)),
            pl.BlockSpec((depth, tile), lambda n: (0, n)),
            pl.BlockSpec((depth, tile), lambda n: (0, tiles + n)),
            pl.BlockSpec((depth, tile), lambda n: (0, 2 * tiles + n)),
        ],
        out_specs=[
            pl.BlockSpec((rows, tile), lambda n: (0, n)),
            pl.BlockSpec((rows, 2 * width), lambda n: (0, 0)),
        ],
        cost_estimate=pl.CostEstimate(
            flops=6 * rows * depth * width,
            bytes_accessed=4 * rows * depth + 6 * depth * width + 6 * rows * width,
            transcendentals=rows * width,
        ),
    )(h2, g_rows, wide, wide, wide)


def scores_of(q, k, seg_q, seg_k, row_base):
    s = lax.dot_general(q, k, (((1,), (1,)), ((), ())), preferred_element_type=F32) * (HD**-0.5)
    rows = lax.broadcasted_iota(jnp.int32, s.shape, 0) + row_base
    cols = lax.broadcasted_iota(jnp.int32, s.shape, 1)
    return jnp.where((seg_q == seg_k) & (rows >= cols), s, MASKED)


def softmax_of(s):
    peak = jnp.max(s, axis=-1, keepdims=True)
    e = jnp.exp(s - peak)
    return e * (1.0 / jnp.sum(e, axis=-1, keepdims=True))


def turn(values, cos, sin):
    return values * cos + pltpu.roll(values, HD // 2, 1) * sin


def attend_kernel(
    blocks, t_ref, q_ref, k_ref, v_ref, segc_ref, segr_ref, cos_ref, sin_ref,
    out_ref, saved_ref, kt, vt,
):
    size = q_ref.shape[0] // blocks
    width = saved_ref.shape[1] // 3
    head = pl.program_id(0) * HD
    t = t_ref[0]

    def rows(block):
        return pl.ds(pl.multiple_of((block ^ t) * size, size), size)

    def lanes(which):
        return pl.ds(pl.multiple_of(which * width + head, HD), HD)

    for b in range(blocks):
        lo, hi = b * size, (b + 1) * size
        cos, sin = cos_ref[lo:hi, :], sin_ref[lo:hi, :]
        q = turn(q_ref[rows(b), :], cos, sin).astype(BF16)
        k = turn(k_ref[rows(b), :], cos, sin).astype(BF16)
        v = v_ref[rows(b), :].astype(BF16)
        saved_ref[rows(b), lanes(0)] = q
        saved_ref[rows(b), lanes(1)] = k
        saved_ref[rows(b), lanes(2)] = v
        kt[lo:hi, :] = k
        vt[lo:hi, :] = v
        s = scores_of(q, kt[:hi, :], segc_ref[lo:hi, :], segr_ref[:, :hi], lo)
        p = softmax_of(s).astype(BF16)
        out_ref[rows(b), :] = jnp.dot(p, vt[:hi, :], preferred_element_type=F32).astype(BF16)


def attend_forward(t, pre, segc, segr, cos, sin):
    rows, width = pre.shape[0], pre.shape[1] // 3
    heads = width // HD
    blocks = lax.axis_size("tensor")
    table = pl.BlockSpec((rows, HD), lambda h, t: (0, 0))

    def kernel(*refs):
        attend_kernel(blocks, *refs)

    return pl.pallas_call(
        kernel,
        out_shape=[
            jax.ShapeDtypeStruct((rows, width), BF16),
            jax.ShapeDtypeStruct((rows, 3 * width), BF16),
        ],
        grid_spec=pltpu.PrefetchScalarGridSpec(
            num_scalar_prefetch=1,
            grid=(heads,),
            in_specs=[
                pl.BlockSpec((rows, HD), lambda h, t: (0, h)),
                pl.BlockSpec((rows, HD), lambda h, t: (0, heads + h)),
                pl.BlockSpec((rows, HD), lambda h, t: (0, 2 * heads + h)),
                pl.BlockSpec((rows, 1), lambda h, t: (0, 0)),
                pl.BlockSpec((1, rows), lambda h, t: (0, 0)),
                table,
                table,
            ],
            out_specs=[
                pl.BlockSpec((rows, HD), lambda h, t: (0, h)),
                pl.BlockSpec((rows, 3 * width), lambda h, t: (0, 0)),
            ],
            scratch_shapes=[pltpu.VMEM((rows, HD), BF16)] * 2,
        ),
        cost_estimate=pl.CostEstimate(
            flops=4 * rows * rows * width,
            bytes_accessed=20 * rows * width,
            transcendentals=rows * rows * heads,
        ),
    )(t, pre, pre, pre, segc, segr, cos, sin)


def unattend_kernel(
    blocks, t_ref, q_ref, k_ref, v_ref, g_ref, segc_ref, segr_ref, cos_ref, sin_ref,
    out_ref, kt, vt, dka, dva,
):
    size = q_ref.shape[0] // blocks
    width = out_ref.shape[1] // 3
    head = pl.program_id(0) * HD
    t = t_ref[0]

    def rows(block):
        return pl.ds(pl.multiple_of((block ^ t) * size, size), size)

    def lanes(which):
        return pl.ds(pl.multiple_of(which * width + head, HD), HD)

    def turn_back(grad, b):
        lo, hi = b * size, (b + 1) * size
        return grad * cos_ref[lo:hi, :] - pltpu.roll(grad, HD // 2, 1) * sin_ref[lo:hi, :]

    for b in range(blocks):
        kt[b * size : (b + 1) * size, :] = k_ref[rows(b), :]
        vt[b * size : (b + 1) * size, :] = v_ref[rows(b), :]
    for b in range(blocks - 1, -1, -1):
        n = (b + 1) * size
        q = q_ref[rows(b), :]
        g = g_ref[rows(b), :]
        s = scores_of(q, kt[:n, :], segc_ref[b * size : n, :], segr_ref[:, :n], b * size)
        p = softmax_of(s)
        dp = lax.dot_general(g, vt[:n, :], (((1,), (1,)), ((), ())), preferred_element_type=F32)
        pdp = p * dp
        delta = jnp.sum(pdp, axis=-1, keepdims=True)
        raw = ((pdp - p * delta) * (HD**-0.5)).astype(BF16)
        dq = jnp.dot(raw, kt[:n, :], preferred_element_type=F32)
        out_ref[rows(b), lanes(0)] = turn_back(dq, b).astype(BF16)
        dk = lax.dot_general(raw, q, (((0,), (0,)), ((), ())), preferred_element_type=F32)
        dv = lax.dot_general(
            p.astype(BF16), g, (((0,), (0,)), ((), ())), preferred_element_type=F32
        )
        if b == blocks - 1:
            dka[...] = dk
            dva[...] = dv
        else:
            dka[:n, :] += dk
            dva[:n, :] += dv
    for b in range(blocks):
        lo, hi = b * size, (b + 1) * size
        out_ref[rows(b), lanes(1)] = turn_back(dka[lo:hi, :], b).astype(BF16)
        out_ref[rows(b), lanes(2)] = dva[lo:hi, :].astype(BF16)


def attend_backward(t, saved, g, segc, segr, cos, sin):
    rows, width = g.shape
    heads = width // HD
    blocks = lax.axis_size("tensor")
    table = pl.BlockSpec((rows, HD), lambda h, t: (0, 0))

    def kernel(*refs):
        unattend_kernel(blocks, *refs)

    return pl.pallas_call(
        kernel,
        out_shape=jax.ShapeDtypeStruct((rows, 3 * width), BF16),
        grid_spec=pltpu.PrefetchScalarGridSpec(
            num_scalar_prefetch=1,
            grid=(heads,),
            in_specs=[
                pl.BlockSpec((rows, HD), lambda h, t: (0, h)),
                pl.BlockSpec((rows, HD), lambda h, t: (0, heads + h)),
                pl.BlockSpec((rows, HD), lambda h, t: (0, 2 * heads + h)),
                pl.BlockSpec((rows, HD), lambda h, t: (0, h)),
                pl.BlockSpec((rows, 1), lambda h, t: (0, 0)),
                pl.BlockSpec((1, rows), lambda h, t: (0, 0)),
                table,
                table,
            ],
            out_specs=pl.BlockSpec((rows, 3 * width), lambda h, t: (0, 0)),
            scratch_shapes=[pltpu.VMEM((rows, HD), BF16)] * 2 + [pltpu.VMEM((rows, HD), F32)] * 2,
        ),
        cost_estimate=pl.CostEstimate(
            flops=10 * rows * rows * width,
            bytes_accessed=14 * rows * width,
            transcendentals=rows * rows * heads,
        ),
    )(t, saved, saved, saved, g, segc, segr, cos, sin)


def per_device(
    tokens,
    lengths,
    query_weight,
    key_weight,
    value_weight,
    output_weight,
    gate_weight,
    up_weight,
    down_weight,
    cotangent,
):
    local = tokens.shape[0]
    group = lax.axis_size("tensor")
    t = lax.axis_index("tensor")
    slot_rows = local * group
    heads_width = query_weight.shape[1]
    hidden_width = gate_weight.shape[1]
    t_arg = t.astype(jnp.int32).reshape(1)

    half = hidden_width // 2

    mixed = gather_dp(
        jnp.concatenate([query_weight, key_weight, value_weight, output_weight.T], axis=1), 0
    )
    heads_full, out_full = mixed[:, : 3 * heads_width], mixed[:, 3 * heads_width :]
    wide = [
        gather_dp(
            jnp.concatenate(
                [w[:, a * half : (a + 1) * half] for w in (gate_weight, up_weight)]
                + [down_weight[a * half : (a + 1) * half].T],
                axis=1,
            ),
            0,
        )
        for a in range(2)
    ]

    segment, position, valid_all = slot_layout(lengths[0], slot_rows)
    valid = lax.dynamic_slice_in_dim(valid_all, t * local, local, 0).astype(F32)[:, None]
    cos, sin = rope_wide(position)
    segc, segr = segment[:, None], segment[None, :]

    residual = tokens.astype(F32)
    grad_out = cotangent.astype(F32) * valid
    normed_one, inverse_one = norm_forward(residual)
    h1, h1_own, h1_peer = gather_rows(normed_one.astype(BF16))
    g_rows, g_own, g_peer = gather_rows(after(grad_out.astype(BF16), h1))

    def rows_of(value, j):
        return value[j * local : (j + 1) * local]

    context, saved = attend_forward(t_arg, dot_plain(h1, heads_full), segc, segr, cos, sin)

    def attention_piece(j, earlier):
        rows = rows_of(context, j)
        return dot_last(rows if earlier is None else after(rows, earlier), out_full)

    middle = residual + scatter_rows(attention_piece)
    normed_two, inverse_two = norm_forward(middle)
    h2, h2_own, h2_peer = gather_rows(normed_two.astype(BF16))

    hidden_0, d_wide_0 = feed(h2, g_rows, wide[0])
    first_grad = pair_sum([(h2_own, h2_peer, d_wide_0), (g_own, g_peer, hidden_0)])
    first_sum = scatter_dp(first_grad)
    d_first = dot_last(d_wide_0, wide[0][:, : 2 * half])
    wide_1, first_grad, d_first = lax.optimization_barrier((wide[1], first_grad, d_first))
    hidden_1, d_wide_1 = feed(h2, g_rows, wide_1)

    def feed_back_piece(j, earlier):
        rows = rows_of(d_wide_1, j)
        rows = rows if earlier is None else after(rows, earlier)
        return rows_of(d_first, j) + dot_last(rows, wide_1[:, : 2 * half])

    d_normed_two = scatter_rows(feed_back_piece)
    d_middle = grad_out + norm_backward(normed_two, inverse_two, d_normed_two)
    second_grad = pair_sum([(h2_own, h2_peer, d_wide_1), (g_own, g_peer, hidden_1)])
    (d_attention, d_attention_own, d_attention_peer), neighbour = gather_steps(d_middle.astype(BF16))
    second_sum = scatter_dp(after(second_grad, first_sum, neighbour))

    d_context = dot_plain(d_attention, out_full).astype(BF16)
    d_pre = attend_backward(t_arg, saved, d_context, segc, segr, cos, sin)
    mixed_grad = pair_sum([(h1_own, h1_peer, d_pre), (d_attention_own, d_attention_peer, context)])
    mixed_sum = scatter_dp(after(mixed_grad, second_sum))

    def feed_piece(j, earlier):
        rows = after(rows_of(hidden_0, j), d_pre if earlier is None else earlier)
        return dot_last(rows, wide[0][:, 2 * half :]) + dot_last(
            rows_of(hidden_1, j), wide_1[:, 2 * half :]
        )

    feed_out = scatter_rows(feed_piece)
    output = (valid * (middle + feed_out)).astype(BF16)

    def heads_back_piece(j, earlier):
        rows = after(rows_of(d_pre, j), mixed_grad if earlier is None else earlier)
        return dot_last(rows, heads_full)

    d_normed_one = scatter_rows(heads_back_piece)
    input_grad = (d_middle + norm_backward(normed_one, inverse_one, d_normed_one)).astype(BF16)
    wide_sum = [first_sum, second_sum]

    return (
        output,
        input_grad,
        mixed_sum[:, :heads_width],
        mixed_sum[:, heads_width : 2 * heads_width],
        mixed_sum[:, 2 * heads_width : 3 * heads_width],
        mixed_sum[:, 3 * heads_width :].T,
        jnp.concatenate([part[:, :half] for part in wide_sum], axis=1),
        jnp.concatenate([part[:, half : 2 * half] for part in wide_sum], axis=1),
        jnp.concatenate([part[:, 2 * half :].T for part in wide_sum], axis=0),
    )


def solution(mesh):
    return jax.shard_map(
        per_device,
        mesh=mesh,
        in_specs=(
            P(("dp", "tensor"), None),
            P("dp", None),
            P("dp", "tensor"),
            P("dp", "tensor"),
            P("dp", "tensor"),
            P("tensor", "dp"),
            P("dp", "tensor"),
            P("dp", "tensor"),
            P("tensor", "dp"),
            P(("dp", "tensor"), None),
        ),
        out_specs=(
            P(("dp", "tensor"), None),
            P(("dp", "tensor"), None),
            P("dp", "tensor"),
            P("dp", "tensor"),
            P("dp", "tensor"),
            P("tensor", "dp"),
            P("dp", "tensor"),
            P("dp", "tensor"),
            P("tensor", "dp"),
        ),
        check_vma=False,
    )
```

```python
import math

import jax
import jax.numpy as jnp
from jax import lax
from jax.experimental import pallas as pl
from jax.experimental.pallas import tpu as pltpu
from jax.sharding import PartitionSpec as P

HD = 128
EPSILON = 1e-05
ROPE_BASE = 10000.0
MASKED = -1e30
F32 = jnp.float32
BF16 = jnp.bfloat16


def norm_forward(rows):
    centre = jnp.mean(rows, axis=-1, keepdims=True)
    centered = rows - centre
    spread = jnp.mean(centered * centered, axis=-1, keepdims=True)
    inverse = lax.rsqrt(spread + EPSILON)
    return centered * inverse, inverse


def norm_backward(normed, inverse, grad):
    mean_grad = jnp.mean(grad, axis=-1, keepdims=True)
    mean_both = jnp.mean(grad * normed, axis=-1, keepdims=True)
    return (grad - mean_grad - normed * mean_both) * inverse


def slot_layout(lengths_row, row_total):
    ends = jnp.cumsum(lengths_row)
    places = jnp.arange(row_total, dtype=jnp.int32)
    segment = jnp.sum((places[:, None] >= ends[None, :]).astype(jnp.int32), axis=1)
    starts = jnp.concatenate([jnp.zeros((1,), jnp.int32), ends])
    picks = jnp.arange(starts.shape[0], dtype=jnp.int32)
    begins = jnp.sum(jnp.where(segment[:, None] == picks[None, :], starts[None, :], 0), axis=1)
    valid = (places < ends[-1]).astype(jnp.int32)
    return segment, places - begins, valid


def rope_wide(position):
    half = HD // 2
    steps = jnp.arange(half, dtype=F32)
    freqs = jnp.exp(steps * (-2.0 * math.log(ROPE_BASE) / HD))
    angles = position.astype(F32)[:, None] * freqs[None, :]
    cosine, sine = jnp.cos(angles), jnp.sin(angles)
    return (
        jnp.concatenate([cosine, cosine], axis=1),
        jnp.concatenate([-sine, sine], axis=1),
    )


def dot_plain(left, right):
    return jnp.dot(left, right, preferred_element_type=F32)


def dot_first(left, right):
    return lax.dot_general(left, right, (((0,), (0,)), ((), ())), preferred_element_type=F32)


def dot_last(left, right):
    return lax.dot_general(left, right, (((1,), (1,)), ((), ())), preferred_element_type=F32)


def after(value, *deps):
    return lax.optimization_barrier((value,) + deps)[0]


def gather_dp(own, axis):
    return lax.all_gather(own, "dp", axis=axis, tiled=True)


def core_swap(value):
    count = lax.axis_size("dp")
    return lax.ppermute(value, "dp", [(k, k ^ 1) for k in range(count)])


def pair_sum(terms):
    others = [core_swap(dot_first(peer, right).astype(BF16)) for own, peer, right in terms]
    sums = [
        (dot_first(own, right) + other.astype(F32)).astype(BF16)
        for (own, peer, right), other in zip(terms, others)
    ]
    return jnp.concatenate(sums, axis=1)


def scatter_dp(pairs):
    count = lax.axis_size("dp")
    groups = [list(range(core, count, 2)) for core in range(2)]
    total = lax.psum_scatter(
        pairs, "dp", scatter_dimension=0, tiled=True, axis_index_groups=groups
    )
    return total.astype(F32)


def flip(value, bits):
    return lax.ppermute(value, "tensor", [(k, k ^ bits) for k in range(lax.axis_size("tensor"))])


def join_kernel(core_ref, *refs):
    out, own, peer = refs[-3:]
    width = own.shape[1]
    mine = pl.multiple_of(core_ref[0] * width, width)
    other = pl.multiple_of((1 - core_ref[0]) * width, width)
    start = 0
    for ref in refs[:-3]:
        rows = slice(start, start + ref.shape[0])
        out[rows, :] = ref[...]
        own[rows, :] = ref[:, pl.ds(mine, width)]
        peer[rows, :] = ref[:, pl.ds(other, width)]
        start += ref.shape[0]


def join(pieces):
    rows = sum(piece.shape[0] for piece in pieces)
    width = pieces[0].shape[1]
    count = lax.axis_size("dp")
    tile = 2 * width // count
    core = (lax.axis_index("dp") % 2).astype(jnp.int32).reshape(1)
    half = pl.BlockSpec((rows, tile // 2), lambda n, c: (0, n))
    return pl.pallas_call(
        join_kernel,
        out_shape=[
            jax.ShapeDtypeStruct((rows, width), pieces[0].dtype),
            jax.ShapeDtypeStruct((rows, width // 2), pieces[0].dtype),
            jax.ShapeDtypeStruct((rows, width // 2), pieces[0].dtype),
        ],
        grid_spec=pltpu.PrefetchScalarGridSpec(
            num_scalar_prefetch=1,
            grid=(count // 2,),
            in_specs=[pl.BlockSpec((piece.shape[0], tile), lambda n, c: (0, n)) for piece in pieces],
            out_specs=[pl.BlockSpec((rows, tile), lambda n, c: (0, n)), half, half],
        ),
        cost_estimate=pl.CostEstimate(flops=0, bytes_accessed=6 * rows * width, transcendentals=0),
    )(core, *pieces)


def gather_rows(own):
    return gather_steps(own)[0]


def gather_steps(own):
    group = lax.axis_size("tensor")
    if group != 4:
        bits = 1
        while bits < group:
            own = jnp.concatenate([own, flip(own, bits)], axis=0)
            bits *= 2
        return join([own]), (own,)
    half = own.shape[0] // 2
    one = flip(own, 1)
    two = flip(own, 2)
    far_top = flip(one[:half], 2)
    far_low = flip(two[half:], 1)
    return join([own, one, two, far_top, far_low]), (one, two)


def scatter_rows(piece):
    group = lax.axis_size("tensor")
    if group != 4:
        parts = [piece(j, None).astype(BF16) for j in range(group)]
        while len(parts) > 1:
            bits = len(parts) // 2
            parts = [
                parts[j].astype(F32) + flip(parts[j + bits].astype(BF16), bits).astype(F32)
                for j in range(bits)
            ]
        return parts[0]
    far = piece(3, None).astype(BF16)
    half = far.shape[0] // 2
    top = flip(far[:half], 1)
    low = flip(far[half:], 2)
    one = piece(1, far).astype(BF16)
    one_top = flip(one[:half], 1)
    two = piece(2, one).astype(BF16)
    two_low = flip(two[half:], 2)
    one_low = flip((one[half:].astype(F32) + low.astype(F32)).astype(BF16), 1)
    two_top = flip((two[:half].astype(F32) + top.astype(F32)).astype(BF16), 2)
    own = lax.optimization_barrier(piece(0, two))
    ones = jnp.concatenate([one_top, one_low], axis=0).astype(F32)
    twos = jnp.concatenate([two_top, two_low], axis=0).astype(F32)
    return own + ones + twos


def feed_kernel(h_ref, g_ref, gate_ref, up_ref, down_ref, hidden_ref, d_ref):
    tile = gate_ref.shape[1]
    lo = pl.program_id(0) * tile
    gate = jnp.dot(h_ref[...], gate_ref[...], preferred_element_type=F32)
    up = jnp.dot(h_ref[...], up_ref[...], preferred_element_type=F32)
    d_hidden = jnp.dot(g_ref[...], down_ref[...], preferred_element_type=F32)
    sg = jax.nn.sigmoid(gate)
    act = gate * sg
    hidden_ref[...] = (act * up).astype(BF16)
    d_gate = d_hidden * up * (sg + act * (1.0 - sg))
    d_ref[:, pl.ds(pl.multiple_of(lo, tile), tile)] = d_gate.astype(BF16)
    d_ref[:, pl.ds(pl.multiple_of(lo + d_ref.shape[1] // 2, tile), tile)] = (d_hidden * act).astype(BF16)


def feed(h2, g_rows, wide):
    rows, depth = h2.shape
    width = wide.shape[1] // 3
    tile = 256
    tiles = width // tile
    return pl.pallas_call(
        feed_kernel,
        out_shape=[
            jax.ShapeDtypeStruct((rows, width), BF16),
            jax.ShapeDtypeStruct((rows, 2 * width), BF16),
        ],
        grid=(tiles,),
        in_specs=[
            pl.BlockSpec((rows, depth), lambda n: (0, 0)),
            pl.BlockSpec((rows, depth), lambda n: (0, 0)),
            pl.BlockSpec((depth, tile), lambda n: (0, n)),
            pl.BlockSpec((depth, tile), lambda n: (0, tiles + n)),
            pl.BlockSpec((depth, tile), lambda n: (0, 2 * tiles + n)),
        ],
        out_specs=[
            pl.BlockSpec((rows, tile), lambda n: (0, n)),
            pl.BlockSpec((rows, 2 * width), lambda n: (0, 0)),
        ],
        cost_estimate=pl.CostEstimate(
            flops=6 * rows * depth * width,
            bytes_accessed=4 * rows * depth + 6 * depth * width + 6 * rows * width,
            transcendentals=rows * width,
        ),
    )(h2, g_rows, wide, wide, wide)


def scores_of(q, k, seg_q, seg_k, row_base):
    s = lax.dot_general(q, k, (((1,), (1,)), ((), ())), preferred_element_type=F32) * (HD**-0.5)
    rows = lax.broadcasted_iota(jnp.int32, s.shape, 0) + row_base
    cols = lax.broadcasted_iota(jnp.int32, s.shape, 1)
    return jnp.where((seg_q == seg_k) & (rows >= cols), s, MASKED)


def softmax_of(s):
    peak = jnp.max(s, axis=-1, keepdims=True)
    e = jnp.exp(s - peak)
    return e * (1.0 / jnp.sum(e, axis=-1, keepdims=True))


def turn(values, cos, sin):
    return values * cos + pltpu.roll(values, HD // 2, 1) * sin


def attend_kernel(
    blocks, t_ref, q_ref, k_ref, v_ref, segc_ref, segr_ref, cos_ref, sin_ref,
    out_ref, saved_ref, kt, vt,
):
    size = q_ref.shape[0] // blocks
    width = saved_ref.shape[1] // 3
    head = pl.program_id(0) * HD
    t = t_ref[0]

    def rows(block):
        return pl.ds(pl.multiple_of((block ^ t) * size, size), size)

    def lanes(which):
        return pl.ds(pl.multiple_of(which * width + head, HD), HD)

    for b in range(blocks):
        lo, hi = b * size, (b + 1) * size
        cos, sin = cos_ref[lo:hi, :], sin_ref[lo:hi, :]
        q = turn(q_ref[rows(b), :], cos, sin).astype(BF16)
        k = turn(k_ref[rows(b), :], cos, sin).astype(BF16)
        v = v_ref[rows(b), :].astype(BF16)
        saved_ref[rows(b), lanes(0)] = q
        saved_ref[rows(b), lanes(1)] = k
        saved_ref[rows(b), lanes(2)] = v
        kt[lo:hi, :] = k
        vt[lo:hi, :] = v
        s = scores_of(q, kt[:hi, :], segc_ref[lo:hi, :], segr_ref[:, :hi], lo)
        p = softmax_of(s).astype(BF16)
        out_ref[rows(b), :] = jnp.dot(p, vt[:hi, :], preferred_element_type=F32).astype(BF16)


def attend_forward(t, pre, segc, segr, cos, sin):
    rows, width = pre.shape[0], pre.shape[1] // 3
    heads = width // HD
    blocks = lax.axis_size("tensor")
    table = pl.BlockSpec((rows, HD), lambda h, t: (0, 0))

    def kernel(*refs):
        attend_kernel(blocks, *refs)

    return pl.pallas_call(
        kernel,
        out_shape=[
            jax.ShapeDtypeStruct((rows, width), BF16),
            jax.ShapeDtypeStruct((rows, 3 * width), BF16),
        ],
        grid_spec=pltpu.PrefetchScalarGridSpec(
            num_scalar_prefetch=1,
            grid=(heads,),
            in_specs=[
                pl.BlockSpec((rows, HD), lambda h, t: (0, h)),
                pl.BlockSpec((rows, HD), lambda h, t: (0, heads + h)),
                pl.BlockSpec((rows, HD), lambda h, t: (0, 2 * heads + h)),
                pl.BlockSpec((rows, 1), lambda h, t: (0, 0)),
                pl.BlockSpec((1, rows), lambda h, t: (0, 0)),
                table,
                table,
            ],
            out_specs=[
                pl.BlockSpec((rows, HD), lambda h, t: (0, h)),
                pl.BlockSpec((rows, 3 * width), lambda h, t: (0, 0)),
            ],
            scratch_shapes=[pltpu.VMEM((rows, HD), BF16)] * 2,
        ),
        cost_estimate=pl.CostEstimate(
            flops=4 * rows * rows * width,
            bytes_accessed=20 * rows * width,
            transcendentals=rows * rows * heads,
        ),
    )(t, pre, pre, pre, segc, segr, cos, sin)


def unattend_kernel(
    blocks, t_ref, q_ref, k_ref, v_ref, g_ref, segc_ref, segr_ref, cos_ref, sin_ref,
    out_ref, kt, vt, dka, dva,
):
    size = q_ref.shape[0] // blocks
    width = out_ref.shape[1] // 3
    head = pl.program_id(0) * HD
    t = t_ref[0]

    def rows(block):
        return pl.ds(pl.multiple_of((block ^ t) * size, size), size)

    def lanes(which):
        return pl.ds(pl.multiple_of(which * width + head, HD), HD)

    def turn_back(grad, b):
        lo, hi = b * size, (b + 1) * size
        return grad * cos_ref[lo:hi, :] - pltpu.roll(grad, HD // 2, 1) * sin_ref[lo:hi, :]

    for b in range(blocks):
        kt[b * size : (b + 1) * size, :] = k_ref[rows(b), :]
        vt[b * size : (b + 1) * size, :] = v_ref[rows(b), :]
    for b in range(blocks - 1, -1, -1):
        n = (b + 1) * size
        q = q_ref[rows(b), :]
        g = g_ref[rows(b), :]
        s = scores_of(q, kt[:n, :], segc_ref[b * size : n, :], segr_ref[:, :n], b * size)
        p = softmax_of(s)
        dp = lax.dot_general(g, vt[:n, :], (((1,), (1,)), ((), ())), preferred_element_type=F32)
        pdp = p * dp
        delta = jnp.sum(pdp, axis=-1, keepdims=True)
        raw = ((pdp - p * delta) * (HD**-0.5)).astype(BF16)
        dq = jnp.dot(raw, kt[:n, :], preferred_element_type=F32)
        out_ref[rows(b), lanes(0)] = turn_back(dq, b).astype(BF16)
        dk = lax.dot_general(raw, q, (((0,), (0,)), ((), ())), preferred_element_type=F32)
        dv = lax.dot_general(
            p.astype(BF16), g, (((0,), (0,)), ((), ())), preferred_element_type=F32
        )
        if b == blocks - 1:
            dka[...] = dk
            dva[...] = dv
        else:
            dka[:n, :] += dk
            dva[:n, :] += dv
    for b in range(blocks):
        lo, hi = b * size, (b + 1) * size
        out_ref[rows(b), lanes(1)] = turn_back(dka[lo:hi, :], b).astype(BF16)
        out_ref[rows(b), lanes(2)] = dva[lo:hi, :].astype(BF16)


def attend_backward(t, saved, g, segc, segr, cos, sin):
    rows, width = g.shape
    heads = width // HD
    blocks = lax.axis_size("tensor")
    table = pl.BlockSpec((rows, HD), lambda h, t: (0, 0))

    def kernel(*refs):
        unattend_kernel(blocks, *refs)

    return pl.pallas_call(
        kernel,
        out_shape=jax.ShapeDtypeStruct((rows, 3 * width), BF16),
        grid_spec=pltpu.PrefetchScalarGridSpec(
            num_scalar_prefetch=1,
            grid=(heads,),
            in_specs=[
                pl.BlockSpec((rows, HD), lambda h, t: (0, h)),
                pl.BlockSpec((rows, HD), lambda h, t: (0, heads + h)),
                pl.BlockSpec((rows, HD), lambda h, t: (0, 2 * heads + h)),
                pl.BlockSpec((rows, HD), lambda h, t: (0, h)),
                pl.BlockSpec((rows, 1), lambda h, t: (0, 0)),
                pl.BlockSpec((1, rows), lambda h, t: (0, 0)),
                table,
                table,
            ],
            out_specs=pl.BlockSpec((rows, 3 * width), lambda h, t: (0, 0)),
            scratch_shapes=[pltpu.VMEM((rows, HD), BF16)] * 2 + [pltpu.VMEM((rows, HD), F32)] * 2,
        ),
        cost_estimate=pl.CostEstimate(
            flops=10 * rows * rows * width,
            bytes_accessed=14 * rows * width,
            transcendentals=rows * rows * heads,
        ),
    )(t, saved, saved, saved, g, segc, segr, cos, sin)


def per_device(
    tokens,
    lengths,
    query_weight,
    key_weight,
    value_weight,
    output_weight,
    gate_weight,
    up_weight,
    down_weight,
    cotangent,
):
    local = tokens.shape[0]
    group = lax.axis_size("tensor")
    t = lax.axis_index("tensor")
    slot_rows = local * group
    heads_width = query_weight.shape[1]
    hidden_width = gate_weight.shape[1]
    t_arg = t.astype(jnp.int32).reshape(1)

    half = hidden_width // 2

    mixed = gather_dp(
        jnp.concatenate([query_weight, key_weight, value_weight, output_weight.T], axis=1), 0
    )
    heads_full, out_full = mixed[:, : 3 * heads_width], mixed[:, 3 * heads_width :]
    wide = [
        gather_dp(
            jnp.concatenate(
                [w[:, a * half : (a + 1) * half] for w in (gate_weight, up_weight)]
                + [down_weight[a * half : (a + 1) * half].T],
                axis=1,
            ),
            0,
        )
        for a in range(2)
    ]

    segment, position, valid_all = slot_layout(lengths[0], slot_rows)
    valid = lax.dynamic_slice_in_dim(valid_all, t * local, local, 0).astype(F32)[:, None]
    cos, sin = rope_wide(position)
    segc, segr = segment[:, None], segment[None, :]

    residual = tokens.astype(F32)
    grad_out = cotangent.astype(F32) * valid
    normed_one, inverse_one = norm_forward(residual)
    h1, h1_own, h1_peer = gather_rows(normed_one.astype(BF16))
    g_rows, g_own, g_peer = gather_rows(after(grad_out.astype(BF16), h1))

    def rows_of(value, j):
        return value[j * local : (j + 1) * local]

    context, saved = attend_forward(t_arg, dot_plain(h1, heads_full), segc, segr, cos, sin)

    def attention_piece(j, earlier):
        rows = rows_of(context, j)
        return dot_last(rows if earlier is None else after(rows, earlier), out_full)

    middle = residual + scatter_rows(attention_piece)
    normed_two, inverse_two = norm_forward(middle)
    h2, h2_own, h2_peer = gather_rows(normed_two.astype(BF16))

    hidden_0, d_wide_0 = feed(h2, g_rows, wide[0])
    first_grad = pair_sum([(h2_own, h2_peer, d_wide_0), (g_own, g_peer, hidden_0)])
    first_sum = scatter_dp(first_grad)
    d_first = dot_last(d_wide_0, wide[0][:, : 2 * half])
    wide_1, first_grad, d_first = lax.optimization_barrier((wide[1], first_grad, d_first))
    hidden_1, d_wide_1 = feed(h2, g_rows, wide_1)

    pieces = []

    def feed_back_piece(j, earlier):
        rows = rows_of(d_wide_1, j)
        rows = rows if earlier is None else after(rows, earlier)
        pieces.append(rows_of(d_first, j) + dot_last(rows, wide_1[:, : 2 * half]))
        return pieces[-1]

    d_normed_two = scatter_rows(feed_back_piece)
    d_middle = grad_out + norm_backward(normed_two, inverse_two, d_normed_two)
    d_wide_1, hidden_1, _ = lax.optimization_barrier((d_wide_1, hidden_1, pieces[-1]))
    second_grad = pair_sum([(h2_own, h2_peer, d_wide_1), (g_own, g_peer, hidden_1)])
    (d_attention, d_attention_own, d_attention_peer), neighbours = gather_steps(d_middle.astype(BF16))
    second_sum = scatter_dp(after(second_grad, first_sum, *neighbours))

    d_context = dot_plain(d_attention, out_full).astype(BF16)
    d_pre = attend_backward(t_arg, saved, d_context, segc, segr, cos, sin)
    mixed_grad = pair_sum([(h1_own, h1_peer, d_pre), (d_attention_own, d_attention_peer, context)])
    mixed_sum = scatter_dp(after(mixed_grad, second_sum))

    def feed_piece(j, earlier):
        rows = after(rows_of(hidden_0, j), d_pre if earlier is None else earlier)
        return dot_last(rows, wide[0][:, 2 * half :]) + dot_last(
            rows_of(hidden_1, j), wide_1[:, 2 * half :]
        )

    feed_out = scatter_rows(feed_piece)
    output = (valid * (middle + feed_out)).astype(BF16)

    def heads_back_piece(j, earlier):
        rows = after(rows_of(d_pre, j), mixed_grad if earlier is None else earlier)
        return dot_last(rows, heads_full)

    d_normed_one = scatter_rows(heads_back_piece)
    input_grad = (d_middle + norm_backward(normed_one, inverse_one, d_normed_one)).astype(BF16)
    wide_sum = [first_sum, second_sum]

    return (
        output,
        input_grad,
        mixed_sum[:, :heads_width],
        mixed_sum[:, heads_width : 2 * heads_width],
        mixed_sum[:, 2 * heads_width : 3 * heads_width],
        mixed_sum[:, 3 * heads_width :].T,
        jnp.concatenate([part[:, :half] for part in wide_sum], axis=1),
        jnp.concatenate([part[:, half : 2 * half] for part in wide_sum], axis=1),
        jnp.concatenate([part[:, 2 * half :].T for part in wide_sum], axis=0),
    )


def solution(mesh):
    return jax.shard_map(
        per_device,
        mesh=mesh,
        in_specs=(
            P(("dp", "tensor"), None),
            P("dp", None),
            P("dp", "tensor"),
            P("dp", "tensor"),
            P("dp", "tensor"),
            P("tensor", "dp"),
            P("dp", "tensor"),
            P("dp", "tensor"),
            P("tensor", "dp"),
            P(("dp", "tensor"), None),
        ),
        out_specs=(
            P(("dp", "tensor"), None),
            P(("dp", "tensor"), None),
            P("dp", "tensor"),
            P("dp", "tensor"),
            P("dp", "tensor"),
            P("tensor", "dp"),
            P("dp", "tensor"),
            P("dp", "tensor"),
            P("tensor", "dp"),
        ),
        check_vma=False,
    )
```

```python
import math

import jax
import jax.numpy as jnp
from jax import lax
from jax.experimental import pallas as pl
from jax.experimental.pallas import tpu as pltpu
from jax.sharding import PartitionSpec as P

HD = 128
EPSILON = 1e-05
ROPE_BASE = 10000.0
MASKED = -1e30
F32 = jnp.float32
BF16 = jnp.bfloat16


def norm_forward(rows):
    centre = jnp.mean(rows, axis=-1, keepdims=True)
    centered = rows - centre
    spread = jnp.mean(centered * centered, axis=-1, keepdims=True)
    inverse = lax.rsqrt(spread + EPSILON)
    return centered * inverse, inverse


def norm_backward(normed, inverse, grad):
    mean_grad = jnp.mean(grad, axis=-1, keepdims=True)
    mean_both = jnp.mean(grad * normed, axis=-1, keepdims=True)
    return (grad - mean_grad - normed * mean_both) * inverse


def slot_layout(lengths_row, row_total):
    ends = jnp.cumsum(lengths_row)
    places = jnp.arange(row_total, dtype=jnp.int32)
    segment = jnp.sum((places[:, None] >= ends[None, :]).astype(jnp.int32), axis=1)
    starts = jnp.concatenate([jnp.zeros((1,), jnp.int32), ends])
    picks = jnp.arange(starts.shape[0], dtype=jnp.int32)
    begins = jnp.sum(jnp.where(segment[:, None] == picks[None, :], starts[None, :], 0), axis=1)
    valid = (places < ends[-1]).astype(jnp.int32)
    return segment, places - begins, valid


def rope_wide(position):
    half = HD // 2
    steps = jnp.arange(half, dtype=F32)
    freqs = jnp.exp(steps * (-2.0 * math.log(ROPE_BASE) / HD))
    angles = position.astype(F32)[:, None] * freqs[None, :]
    cosine, sine = jnp.cos(angles), jnp.sin(angles)
    return (
        jnp.concatenate([cosine, cosine], axis=1),
        jnp.concatenate([-sine, sine], axis=1),
    )


def dot_plain(left, right):
    return jnp.dot(left, right, preferred_element_type=F32)


def dot_first(left, right):
    return lax.dot_general(left, right, (((0,), (0,)), ((), ())), preferred_element_type=F32)


def dot_last(left, right):
    return lax.dot_general(left, right, (((1,), (1,)), ((), ())), preferred_element_type=F32)


def after(value, *deps):
    return lax.optimization_barrier((value,) + deps)[0]


def gather_dp(own, axis):
    return lax.all_gather(own, "dp", axis=axis, tiled=True)


def core_swap(value):
    count = lax.axis_size("dp")
    return lax.ppermute(value, "dp", [(k, k ^ 1) for k in range(count)])


def pair_sum(terms):
    others = [core_swap(dot_first(peer, right).astype(BF16)) for own, peer, right in terms]
    sums = [
        (dot_first(own, right) + other.astype(F32)).astype(BF16)
        for (own, peer, right), other in zip(terms, others)
    ]
    return jnp.concatenate(sums, axis=1)


def scatter_dp(pairs):
    count = lax.axis_size("dp")
    groups = [list(range(core, count, 2)) for core in range(2)]
    return lax.psum_scatter(
        pairs, "dp", scatter_dimension=0, tiled=True, axis_index_groups=groups
    )


def pack_kernel(q_ref, k_ref, v_ref, o_ref, out_ref):
    width = q_ref.shape[1]
    for n, ref in enumerate((q_ref, k_ref, v_ref)):
        out_ref[:, n * width : (n + 1) * width] = ref[...]
    out_ref[:, 3 * width :] = o_ref[...].astype(F32).T.astype(BF16)


def pack_mixed(query, key, value, output):
    rows, width = query.shape
    tile = min(rows, 128)
    plain = pl.BlockSpec((tile, width), lambda n: (n, 0))
    return pl.pallas_call(
        pack_kernel,
        out_shape=jax.ShapeDtypeStruct((rows, 4 * width), BF16),
        grid=(rows // tile,),
        in_specs=[plain, plain, plain, pl.BlockSpec((width, tile), lambda n: (0, n))],
        out_specs=pl.BlockSpec((tile, 4 * width), lambda n: (n, 0)),
        cost_estimate=pl.CostEstimate(flops=0, bytes_accessed=16 * rows * width, transcendentals=0),
    )(query, key, value, output)


def split_kernel(in_ref, q_ref, k_ref, v_ref, o_ref):
    width = q_ref.shape[1]
    for n, ref in enumerate((q_ref, k_ref, v_ref)):
        ref[...] = in_ref[:, n * width : (n + 1) * width].astype(F32)
    o_ref[...] = in_ref[:, 3 * width :].astype(F32).T


def split_mixed(total):
    rows, width = total.shape[0], total.shape[1] // 4
    tile = min(rows, 128)
    plain = pl.BlockSpec((tile, width), lambda n: (n, 0))
    return pl.pallas_call(
        split_kernel,
        out_shape=[jax.ShapeDtypeStruct((rows, width), F32)] * 3
        + [jax.ShapeDtypeStruct((width, rows), F32)],
        grid=(rows // tile,),
        in_specs=[pl.BlockSpec((tile, 4 * width), lambda n: (n, 0))],
        out_specs=[plain, plain, plain, pl.BlockSpec((width, tile), lambda n: (0, n))],
        cost_estimate=pl.CostEstimate(flops=0, bytes_accessed=6 * total.size, transcendentals=0),
    )(total)


def flip(value, bits):
    return lax.ppermute(value, "tensor", [(k, k ^ bits) for k in range(lax.axis_size("tensor"))])


def join_kernel(core_ref, *refs):
    out, own, peer = refs[-3:]
    width = own.shape[1]
    mine = pl.multiple_of(core_ref[0] * width, width)
    other = pl.multiple_of((1 - core_ref[0]) * width, width)
    start = 0
    for ref in refs[:-3]:
        rows = slice(start, start + ref.shape[0])
        out[rows, :] = ref[...]
        own[rows, :] = ref[:, pl.ds(mine, width)]
        peer[rows, :] = ref[:, pl.ds(other, width)]
        start += ref.shape[0]


def join(pieces):
    rows = sum(piece.shape[0] for piece in pieces)
    width = pieces[0].shape[1]
    count = lax.axis_size("dp")
    tile = 2 * width // count
    core = (lax.axis_index("dp") % 2).astype(jnp.int32).reshape(1)
    half = pl.BlockSpec((rows, tile // 2), lambda n, c: (0, n))
    return pl.pallas_call(
        join_kernel,
        out_shape=[
            jax.ShapeDtypeStruct((rows, width), pieces[0].dtype),
            jax.ShapeDtypeStruct((rows, width // 2), pieces[0].dtype),
            jax.ShapeDtypeStruct((rows, width // 2), pieces[0].dtype),
        ],
        grid_spec=pltpu.PrefetchScalarGridSpec(
            num_scalar_prefetch=1,
            grid=(count // 2,),
            in_specs=[pl.BlockSpec((piece.shape[0], tile), lambda n, c: (0, n)) for piece in pieces],
            out_specs=[pl.BlockSpec((rows, tile), lambda n, c: (0, n)), half, half],
        ),
        cost_estimate=pl.CostEstimate(flops=0, bytes_accessed=6 * rows * width, transcendentals=0),
    )(core, *pieces)


def gather_rows(own):
    return gather_steps(own)[0]


def gather_steps(own):
    group = lax.axis_size("tensor")
    if group != 4:
        bits = 1
        while bits < group:
            own = jnp.concatenate([own, flip(own, bits)], axis=0)
            bits *= 2
        return join([own]), (own,)
    half = own.shape[0] // 2
    one = flip(own, 1)
    two = flip(own, 2)
    far_top = flip(one[:half], 2)
    far_low = flip(two[half:], 1)
    return join([own, one, two, far_top, far_low]), (one, two)


def scatter_rows(piece):
    group = lax.axis_size("tensor")
    if group != 4:
        parts = [piece(j, None).astype(BF16) for j in range(group)]
        while len(parts) > 1:
            bits = len(parts) // 2
            parts = [
                parts[j].astype(F32) + flip(parts[j + bits].astype(BF16), bits).astype(F32)
                for j in range(bits)
            ]
        return parts[0]
    far = piece(3, None).astype(BF16)
    half = far.shape[0] // 2
    top = flip(far[:half], 1)
    low = flip(far[half:], 2)
    one = piece(1, far).astype(BF16)
    one_top = flip(one[:half], 1)
    two = piece(2, one).astype(BF16)
    two_low = flip(two[half:], 2)
    one_low = flip((one[half:].astype(F32) + low.astype(F32)).astype(BF16), 1)
    two_top = flip((two[:half].astype(F32) + top.astype(F32)).astype(BF16), 2)
    own = lax.optimization_barrier(piece(0, two))
    ones = jnp.concatenate([one_top, one_low], axis=0).astype(F32)
    twos = jnp.concatenate([two_top, two_low], axis=0).astype(F32)
    return own + ones + twos


def feed_kernel(h_ref, g_ref, gate_ref, up_ref, down_ref, hidden_ref, d_ref):
    tile = gate_ref.shape[1]
    lo = pl.program_id(0) * tile
    gate = jnp.dot(h_ref[...], gate_ref[...], preferred_element_type=F32)
    up = jnp.dot(h_ref[...], up_ref[...], preferred_element_type=F32)
    d_hidden = jnp.dot(g_ref[...], down_ref[...], preferred_element_type=F32)
    sg = jax.nn.sigmoid(gate)
    act = gate * sg
    hidden_ref[...] = (act * up).astype(BF16)
    d_gate = d_hidden * up * (sg + act * (1.0 - sg))
    d_ref[:, pl.ds(pl.multiple_of(lo, tile), tile)] = d_gate.astype(BF16)
    d_ref[:, pl.ds(pl.multiple_of(lo + d_ref.shape[1] // 2, tile), tile)] = (d_hidden * act).astype(BF16)


def feed(h2, g_rows, wide):
    rows, depth = h2.shape
    width = wide.shape[1] // 3
    tile = 256
    tiles = width // tile
    return pl.pallas_call(
        feed_kernel,
        out_shape=[
            jax.ShapeDtypeStruct((rows, width), BF16),
            jax.ShapeDtypeStruct((rows, 2 * width), BF16),
        ],
        grid=(tiles,),
        in_specs=[
            pl.BlockSpec((rows, depth), lambda n: (0, 0)),
            pl.BlockSpec((rows, depth), lambda n: (0, 0)),
            pl.BlockSpec((depth, tile), lambda n: (0, n)),
            pl.BlockSpec((depth, tile), lambda n: (0, tiles + n)),
            pl.BlockSpec((depth, tile), lambda n: (0, 2 * tiles + n)),
        ],
        out_specs=[
            pl.BlockSpec((rows, tile), lambda n: (0, n)),
            pl.BlockSpec((rows, 2 * width), lambda n: (0, 0)),
        ],
        cost_estimate=pl.CostEstimate(
            flops=6 * rows * depth * width,
            bytes_accessed=4 * rows * depth + 6 * depth * width + 6 * rows * width,
            transcendentals=rows * width,
        ),
    )(h2, g_rows, wide, wide, wide)


def scores_of(q, k, seg_q, seg_k, row_base):
    s = lax.dot_general(q, k, (((1,), (1,)), ((), ())), preferred_element_type=F32) * (HD**-0.5)
    rows = lax.broadcasted_iota(jnp.int32, s.shape, 0) + row_base
    cols = lax.broadcasted_iota(jnp.int32, s.shape, 1)
    return jnp.where((seg_q == seg_k) & (rows >= cols), s, MASKED)


def softmax_of(s):
    peak = jnp.max(s, axis=-1, keepdims=True)
    e = jnp.exp(s - peak)
    return e * (1.0 / jnp.sum(e, axis=-1, keepdims=True))


def turn(values, cos, sin):
    return values * cos + pltpu.roll(values, HD // 2, 1) * sin


def attend_kernel(
    blocks, t_ref, q_ref, k_ref, v_ref, segc_ref, segr_ref, cos_ref, sin_ref,
    out_ref, saved_ref, kt, vt,
):
    size = q_ref.shape[0] // blocks
    width = saved_ref.shape[1] // 3
    head = pl.program_id(0) * HD
    t = t_ref[0]

    def rows(block):
        return pl.ds(pl.multiple_of((block ^ t) * size, size), size)

    def lanes(which):
        return pl.ds(pl.multiple_of(which * width + head, HD), HD)

    for b in range(blocks):
        lo, hi = b * size, (b + 1) * size
        cos, sin = cos_ref[lo:hi, :], sin_ref[lo:hi, :]
        q = turn(q_ref[rows(b), :], cos, sin).astype(BF16)
        k = turn(k_ref[rows(b), :], cos, sin).astype(BF16)
        v = v_ref[rows(b), :].astype(BF16)
        saved_ref[rows(b), lanes(0)] = q
        saved_ref[rows(b), lanes(1)] = k
        saved_ref[rows(b), lanes(2)] = v
        kt[lo:hi, :] = k
        vt[lo:hi, :] = v
        s = scores_of(q, kt[:hi, :], segc_ref[lo:hi, :], segr_ref[:, :hi], lo)
        p = softmax_of(s).astype(BF16)
        out_ref[rows(b), :] = jnp.dot(p, vt[:hi, :], preferred_element_type=F32).astype(BF16)


def attend_forward(t, pre, segc, segr, cos, sin):
    rows, width = pre.shape[0], pre.shape[1] // 3
    heads = width // HD
    blocks = lax.axis_size("tensor")
    table = pl.BlockSpec((rows, HD), lambda h, t: (0, 0))

    def kernel(*refs):
        attend_kernel(blocks, *refs)

    return pl.pallas_call(
        kernel,
        out_shape=[
            jax.ShapeDtypeStruct((rows, width), BF16),
            jax.ShapeDtypeStruct((rows, 3 * width), BF16),
        ],
        grid_spec=pltpu.PrefetchScalarGridSpec(
            num_scalar_prefetch=1,
            grid=(heads,),
            in_specs=[
                pl.BlockSpec((rows, HD), lambda h, t: (0, h)),
                pl.BlockSpec((rows, HD), lambda h, t: (0, heads + h)),
                pl.BlockSpec((rows, HD), lambda h, t: (0, 2 * heads + h)),
                pl.BlockSpec((rows, 1), lambda h, t: (0, 0)),
                pl.BlockSpec((1, rows), lambda h, t: (0, 0)),
                table,
                table,
            ],
            out_specs=[
                pl.BlockSpec((rows, HD), lambda h, t: (0, h)),
                pl.BlockSpec((rows, 3 * width), lambda h, t: (0, 0)),
            ],
            scratch_shapes=[pltpu.VMEM((rows, HD), BF16)] * 2,
        ),
        cost_estimate=pl.CostEstimate(
            flops=4 * rows * rows * width,
            bytes_accessed=20 * rows * width,
            transcendentals=rows * rows * heads,
        ),
    )(t, pre, pre, pre, segc, segr, cos, sin)


def unattend_kernel(
    blocks, t_ref, q_ref, k_ref, v_ref, g_ref, segc_ref, segr_ref, cos_ref, sin_ref,
    out_ref, kt, vt, dka, dva,
):
    size = q_ref.shape[0] // blocks
    width = out_ref.shape[1] // 3
    head = pl.program_id(0) * HD
    t = t_ref[0]

    def rows(block):
        return pl.ds(pl.multiple_of((block ^ t) * size, size), size)

    def lanes(which):
        return pl.ds(pl.multiple_of(which * width + head, HD), HD)

    def turn_back(grad, b):
        lo, hi = b * size, (b + 1) * size
        return grad * cos_ref[lo:hi, :] - pltpu.roll(grad, HD // 2, 1) * sin_ref[lo:hi, :]

    for b in range(blocks):
        kt[b * size : (b + 1) * size, :] = k_ref[rows(b), :]
        vt[b * size : (b + 1) * size, :] = v_ref[rows(b), :]
    for b in range(blocks - 1, -1, -1):
        n = (b + 1) * size
        q = q_ref[rows(b), :]
        g = g_ref[rows(b), :]
        s = scores_of(q, kt[:n, :], segc_ref[b * size : n, :], segr_ref[:, :n], b * size)
        p = softmax_of(s)
        dp = lax.dot_general(g, vt[:n, :], (((1,), (1,)), ((), ())), preferred_element_type=F32)
        pdp = p * dp
        delta = jnp.sum(pdp, axis=-1, keepdims=True)
        raw = ((pdp - p * delta) * (HD**-0.5)).astype(BF16)
        dq = jnp.dot(raw, kt[:n, :], preferred_element_type=F32)
        out_ref[rows(b), lanes(0)] = turn_back(dq, b).astype(BF16)
        dk = lax.dot_general(raw, q, (((0,), (0,)), ((), ())), preferred_element_type=F32)
        dv = lax.dot_general(
            p.astype(BF16), g, (((0,), (0,)), ((), ())), preferred_element_type=F32
        )
        if b == blocks - 1:
            dka[...] = dk
            dva[...] = dv
        else:
            dka[:n, :] += dk
            dva[:n, :] += dv
    for b in range(blocks):
        lo, hi = b * size, (b + 1) * size
        out_ref[rows(b), lanes(1)] = turn_back(dka[lo:hi, :], b).astype(BF16)
        out_ref[rows(b), lanes(2)] = dva[lo:hi, :].astype(BF16)


def attend_backward(t, saved, g, segc, segr, cos, sin):
    rows, width = g.shape
    heads = width // HD
    blocks = lax.axis_size("tensor")
    table = pl.BlockSpec((rows, HD), lambda h, t: (0, 0))

    def kernel(*refs):
        unattend_kernel(blocks, *refs)

    return pl.pallas_call(
        kernel,
        out_shape=jax.ShapeDtypeStruct((rows, 3 * width), BF16),
        grid_spec=pltpu.PrefetchScalarGridSpec(
            num_scalar_prefetch=1,
            grid=(heads,),
            in_specs=[
                pl.BlockSpec((rows, HD), lambda h, t: (0, h)),
                pl.BlockSpec((rows, HD), lambda h, t: (0, heads + h)),
                pl.BlockSpec((rows, HD), lambda h, t: (0, 2 * heads + h)),
                pl.BlockSpec((rows, HD), lambda h, t: (0, h)),
                pl.BlockSpec((rows, 1), lambda h, t: (0, 0)),
                pl.BlockSpec((1, rows), lambda h, t: (0, 0)),
                table,
                table,
            ],
            out_specs=pl.BlockSpec((rows, 3 * width), lambda h, t: (0, 0)),
            scratch_shapes=[pltpu.VMEM((rows, HD), BF16)] * 2 + [pltpu.VMEM((rows, HD), F32)] * 2,
        ),
        cost_estimate=pl.CostEstimate(
            flops=10 * rows * rows * width,
            bytes_accessed=14 * rows * width,
            transcendentals=rows * rows * heads,
        ),
    )(t, saved, saved, saved, g, segc, segr, cos, sin)


def per_device(
    tokens,
    lengths,
    query_weight,
    key_weight,
    value_weight,
    output_weight,
    gate_weight,
    up_weight,
    down_weight,
    cotangent,
):
    local = tokens.shape[0]
    group = lax.axis_size("tensor")
    t = lax.axis_index("tensor")
    slot_rows = local * group
    heads_width = query_weight.shape[1]
    hidden_width = gate_weight.shape[1]
    t_arg = t.astype(jnp.int32).reshape(1)

    half = hidden_width // 2

    mixed_own = pack_mixed(query_weight, key_weight, value_weight, output_weight)
    mixed_own, gate_weight, up_weight, down_weight = lax.optimization_barrier(
        (mixed_own, gate_weight, up_weight, down_weight)
    )
    mixed = gather_dp(mixed_own, 0)
    heads_full, out_full = mixed[:, : 3 * heads_width], mixed[:, 3 * heads_width :]
    wide = [
        gather_dp(
            jnp.concatenate(
                [w[:, a * half : (a + 1) * half] for w in (gate_weight, up_weight)]
                + [down_weight[a * half : (a + 1) * half].T],
                axis=1,
            ),
            0,
        )
        for a in range(2)
    ]

    segment, position, valid_all = slot_layout(lengths[0], slot_rows)
    valid = lax.dynamic_slice_in_dim(valid_all, t * local, local, 0).astype(F32)[:, None]
    cos, sin = rope_wide(position)
    segc, segr = segment[:, None], segment[None, :]

    residual = tokens.astype(F32)
    grad_out = cotangent.astype(F32) * valid
    normed_one, inverse_one = norm_forward(residual)
    h1, h1_own, h1_peer = gather_rows(normed_one.astype(BF16))
    g_rows, g_own, g_peer = gather_rows(after(grad_out.astype(BF16), h1))

    def rows_of(value, j):
        return value[j * local : (j + 1) * local]

    context, saved = attend_forward(t_arg, dot_plain(h1, heads_full), segc, segr, cos, sin)

    def attention_piece(j, earlier):
        rows = rows_of(context, j)
        return dot_last(rows if earlier is None else after(rows, earlier), out_full)

    middle = residual + scatter_rows(attention_piece)
    normed_two, inverse_two = norm_forward(middle)
    h2, h2_own, h2_peer = gather_rows(normed_two.astype(BF16))

    hidden_0, d_wide_0 = feed(h2, g_rows, wide[0])
    first_grad = pair_sum([(h2_own, h2_peer, d_wide_0), (g_own, g_peer, hidden_0)])
    first_sum = scatter_dp(first_grad)
    d_first = dot_last(d_wide_0, wide[0][:, : 2 * half])
    wide_1, first_grad, d_first = lax.optimization_barrier((wide[1], first_grad, d_first))
    hidden_1, d_wide_1 = feed(h2, g_rows, wide_1)

    pieces = []

    def feed_back_piece(j, earlier):
        rows = rows_of(d_wide_1, j)
        rows = rows if earlier is None else after(rows, earlier)
        pieces.append(rows_of(d_first, j) + dot_last(rows, wide_1[:, : 2 * half]))
        return pieces[-1]

    d_normed_two = scatter_rows(feed_back_piece)
    d_middle = grad_out + norm_backward(normed_two, inverse_two, d_normed_two)
    d_wide_1, hidden_1, _ = lax.optimization_barrier((d_wide_1, hidden_1, pieces[-1]))
    second_grad = pair_sum([(h2_own, h2_peer, d_wide_1), (g_own, g_peer, hidden_1)])
    (d_attention, d_attention_own, d_attention_peer), neighbours = gather_steps(d_middle.astype(BF16))
    second_sum = scatter_dp(after(second_grad, first_sum, *neighbours))

    d_context = dot_plain(d_attention, out_full).astype(BF16)
    d_pre = attend_backward(t_arg, saved, d_context, segc, segr, cos, sin)
    mixed_grad = pair_sum([(h1_own, h1_peer, d_pre), (d_attention_own, d_attention_peer, context)])
    mixed_sum = scatter_dp(after(mixed_grad, second_sum))

    def feed_piece(j, earlier):
        rows = after(rows_of(hidden_0, j), d_pre if earlier is None else earlier)
        return dot_last(rows, wide[0][:, 2 * half :]) + dot_last(
            rows_of(hidden_1, j), wide_1[:, 2 * half :]
        )

    feed_out = scatter_rows(feed_piece)
    output = (valid * (middle + feed_out)).astype(BF16)

    def heads_back_piece(j, earlier):
        rows = after(rows_of(d_pre, j), mixed_grad if earlier is None else earlier)
        return dot_last(rows, heads_full)

    d_normed_one = scatter_rows(heads_back_piece)
    input_grad = (d_middle + norm_backward(normed_one, inverse_one, d_normed_one)).astype(BF16)
    wide_sum = [first_sum.astype(F32), second_sum.astype(F32)]

    return (
        output,
        input_grad,
        *split_mixed(mixed_sum),
        jnp.concatenate([part[:, :half] for part in wide_sum], axis=1),
        jnp.concatenate([part[:, half : 2 * half] for part in wide_sum], axis=1),
        jnp.concatenate([part[:, 2 * half :].T for part in wide_sum], axis=0),
    )


def solution(mesh):
    return jax.shard_map(
        per_device,
        mesh=mesh,
        in_specs=(
            P(("dp", "tensor"), None),
            P("dp", None),
            P("dp", "tensor"),
            P("dp", "tensor"),
            P("dp", "tensor"),
            P("tensor", "dp"),
            P("dp", "tensor"),
            P("dp", "tensor"),
            P("tensor", "dp"),
            P(("dp", "tensor"), None),
        ),
        out_specs=(
            P(("dp", "tensor"), None),
            P(("dp", "tensor"), None),
            P("dp", "tensor"),
            P("dp", "tensor"),
            P("dp", "tensor"),
            P("tensor", "dp"),
            P("dp", "tensor"),
            P("dp", "tensor"),
            P("tensor", "dp"),
        ),
        check_vma=False,
    )
```

```python
import math

import jax
import jax.numpy as jnp
from jax import lax
from jax.experimental import pallas as pl
from jax.experimental.pallas import tpu as pltpu
from jax.sharding import PartitionSpec as P

HD = 128
EPSILON = 1e-05
ROPE_BASE = 10000.0
MASKED = -1e30
F32 = jnp.float32
BF16 = jnp.bfloat16


def norm_forward(rows):
    centre = jnp.mean(rows, axis=-1, keepdims=True)
    centered = rows - centre
    spread = jnp.mean(centered * centered, axis=-1, keepdims=True)
    inverse = lax.rsqrt(spread + EPSILON)
    return centered * inverse, inverse


def norm_backward(normed, inverse, grad):
    mean_grad = jnp.mean(grad, axis=-1, keepdims=True)
    mean_both = jnp.mean(grad * normed, axis=-1, keepdims=True)
    return (grad - mean_grad - normed * mean_both) * inverse


def slot_layout(lengths_row, row_total):
    ends = jnp.cumsum(lengths_row)
    places = jnp.arange(row_total, dtype=jnp.int32)
    segment = jnp.sum((places[:, None] >= ends[None, :]).astype(jnp.int32), axis=1)
    starts = jnp.concatenate([jnp.zeros((1,), jnp.int32), ends])
    picks = jnp.arange(starts.shape[0], dtype=jnp.int32)
    begins = jnp.sum(jnp.where(segment[:, None] == picks[None, :], starts[None, :], 0), axis=1)
    valid = (places < ends[-1]).astype(jnp.int32)
    return segment, places - begins, valid


def rope_wide(position):
    half = HD // 2
    steps = jnp.arange(half, dtype=F32)
    freqs = jnp.exp(steps * (-2.0 * math.log(ROPE_BASE) / HD))
    angles = position.astype(F32)[:, None] * freqs[None, :]
    cosine, sine = jnp.cos(angles), jnp.sin(angles)
    return (
        jnp.concatenate([cosine, cosine], axis=1),
        jnp.concatenate([-sine, sine], axis=1),
    )


def dot_plain(left, right):
    return jnp.dot(left, right, preferred_element_type=F32)


def dot_first(left, right):
    return lax.dot_general(left, right, (((0,), (0,)), ((), ())), preferred_element_type=F32)


def dot_last(left, right):
    return lax.dot_general(left, right, (((1,), (1,)), ((), ())), preferred_element_type=F32)


def after(value, *deps):
    return lax.optimization_barrier((value,) + deps)[0]


def gather_dp(own, axis):
    return lax.all_gather(own, "dp", axis=axis, tiled=True)


def core_swap(value):
    count = lax.axis_size("dp")
    return lax.ppermute(value, "dp", [(k, k ^ 1) for k in range(count)])


def pair_sum(terms):
    others = [core_swap(dot_first(peer, right).astype(BF16)) for own, peer, right in terms]
    sums = [
        (dot_first(own, right) + other.astype(F32)).astype(BF16)
        for (own, peer, right), other in zip(terms, others)
    ]
    return jnp.concatenate(sums, axis=1)


def scatter_dp(pairs):
    count = lax.axis_size("dp")
    groups = [list(range(core, count, 2)) for core in range(2)]
    return lax.psum_scatter(
        pairs, "dp", scatter_dimension=0, tiled=True, axis_index_groups=groups
    )


def pack_kernel(q_ref, k_ref, v_ref, o_ref, out_ref):
    width = q_ref.shape[1]
    for n, ref in enumerate((q_ref, k_ref, v_ref)):
        out_ref[:, n * width : (n + 1) * width] = ref[...]
    out_ref[:, 3 * width :] = o_ref[...].astype(F32).T.astype(BF16)


def pack_mixed(query, key, value, output):
    rows, width = query.shape
    tile = min(rows, 128)
    plain = pl.BlockSpec((tile, width), lambda n: (n, 0))
    return pl.pallas_call(
        pack_kernel,
        out_shape=jax.ShapeDtypeStruct((rows, 4 * width), BF16),
        grid=(rows // tile,),
        in_specs=[plain, plain, plain, pl.BlockSpec((width, tile), lambda n: (0, n))],
        out_specs=pl.BlockSpec((tile, 4 * width), lambda n: (n, 0)),
        cost_estimate=pl.CostEstimate(flops=0, bytes_accessed=16 * rows * width, transcendentals=0),
    )(query, key, value, output)


def split_kernel(in_ref, q_ref, k_ref, v_ref, o_ref):
    width = q_ref.shape[1]
    for n, ref in enumerate((q_ref, k_ref, v_ref)):
        ref[...] = in_ref[:, n * width : (n + 1) * width].astype(F32)
    o_ref[...] = in_ref[:, 3 * width :].astype(F32).T


def split_mixed(total):
    rows, width = total.shape[0], total.shape[1] // 4
    tile = min(rows, 128)
    plain = pl.BlockSpec((tile, width), lambda n: (n, 0))
    return pl.pallas_call(
        split_kernel,
        out_shape=[jax.ShapeDtypeStruct((rows, width), F32)] * 3
        + [jax.ShapeDtypeStruct((width, rows), F32)],
        grid=(rows // tile,),
        in_specs=[pl.BlockSpec((tile, 4 * width), lambda n: (n, 0))],
        out_specs=[plain, plain, plain, pl.BlockSpec((width, tile), lambda n: (0, n))],
        cost_estimate=pl.CostEstimate(flops=0, bytes_accessed=6 * total.size, transcendentals=0),
    )(total)


def flip(value, bits):
    return lax.ppermute(value, "tensor", [(k, k ^ bits) for k in range(lax.axis_size("tensor"))])


def join_kernel(core_ref, *refs):
    out, own, peer = refs[-3:]
    width = own.shape[1]
    mine = pl.multiple_of(core_ref[0] * width, width)
    other = pl.multiple_of((1 - core_ref[0]) * width, width)
    start = 0
    for ref in refs[:-3]:
        rows = slice(start, start + ref.shape[0])
        out[rows, :] = ref[...]
        own[rows, :] = ref[:, pl.ds(mine, width)]
        peer[rows, :] = ref[:, pl.ds(other, width)]
        start += ref.shape[0]


def join(pieces):
    rows = sum(piece.shape[0] for piece in pieces)
    width = pieces[0].shape[1]
    count = lax.axis_size("dp")
    tile = 2 * width // count
    core = (lax.axis_index("dp") % 2).astype(jnp.int32).reshape(1)
    half = pl.BlockSpec((rows, tile // 2), lambda n, c: (0, n))
    return pl.pallas_call(
        join_kernel,
        out_shape=[
            jax.ShapeDtypeStruct((rows, width), pieces[0].dtype),
            jax.ShapeDtypeStruct((rows, width // 2), pieces[0].dtype),
            jax.ShapeDtypeStruct((rows, width // 2), pieces[0].dtype),
        ],
        grid_spec=pltpu.PrefetchScalarGridSpec(
            num_scalar_prefetch=1,
            grid=(count // 2,),
            in_specs=[pl.BlockSpec((piece.shape[0], tile), lambda n, c: (0, n)) for piece in pieces],
            out_specs=[pl.BlockSpec((rows, tile), lambda n, c: (0, n)), half, half],
        ),
        cost_estimate=pl.CostEstimate(flops=0, bytes_accessed=6 * rows * width, transcendentals=0),
    )(core, *pieces)


def gather_rows(own):
    return gather_steps(own)[0]


def gather_steps(own):
    group = lax.axis_size("tensor")
    if group != 4:
        bits = 1
        while bits < group:
            own = jnp.concatenate([own, flip(own, bits)], axis=0)
            bits *= 2
        return join([own]), (own,)
    half = own.shape[0] // 2
    one = flip(own, 1)
    two = flip(own, 2)
    far_top = flip(one[:half], 2)
    far_low = flip(two[half:], 1)
    return join([own, one, two, far_top, far_low]), (one, two)


def scatter_rows(piece):
    group = lax.axis_size("tensor")
    if group != 4:
        parts = [piece(j, None).astype(BF16) for j in range(group)]
        while len(parts) > 1:
            bits = len(parts) // 2
            parts = [
                parts[j].astype(F32) + flip(parts[j + bits].astype(BF16), bits).astype(F32)
                for j in range(bits)
            ]
        return parts[0]
    far = piece(3, None).astype(BF16)
    half = far.shape[0] // 2
    top = flip(far[:half], 1)
    low = flip(far[half:], 2)
    one = piece(1, far).astype(BF16)
    one_top = flip(one[:half], 1)
    two = piece(2, one).astype(BF16)
    two_low = flip(two[half:], 2)
    one_low = flip((one[half:].astype(F32) + low.astype(F32)).astype(BF16), 1)
    two_top = flip((two[:half].astype(F32) + top.astype(F32)).astype(BF16), 2)
    own = lax.optimization_barrier(piece(0, two))
    ones = jnp.concatenate([one_top, one_low], axis=0).astype(F32)
    twos = jnp.concatenate([two_top, two_low], axis=0).astype(F32)
    return own + ones + twos


def feed_kernel(h_ref, g_ref, gate_ref, up_ref, down_ref, hidden_ref, d_ref):
    tile = gate_ref.shape[1]
    lo = pl.program_id(0) * tile
    gate = jnp.dot(h_ref[...], gate_ref[...], preferred_element_type=F32)
    up = jnp.dot(h_ref[...], up_ref[...], preferred_element_type=F32)
    d_hidden = jnp.dot(g_ref[...], down_ref[...], preferred_element_type=F32)
    sg = jax.nn.sigmoid(gate)
    act = gate * sg
    hidden_ref[...] = (act * up).astype(BF16)
    d_gate = d_hidden * up * (sg + act * (1.0 - sg))
    d_ref[:, pl.ds(pl.multiple_of(lo, tile), tile)] = d_gate.astype(BF16)
    d_ref[:, pl.ds(pl.multiple_of(lo + d_ref.shape[1] // 2, tile), tile)] = (d_hidden * act).astype(BF16)


def feed(h2, g_rows, wide):
    rows, depth = h2.shape
    width = wide.shape[1] // 3
    tile = 256
    tiles = width // tile
    return pl.pallas_call(
        feed_kernel,
        out_shape=[
            jax.ShapeDtypeStruct((rows, width), BF16),
            jax.ShapeDtypeStruct((rows, 2 * width), BF16),
        ],
        grid=(tiles,),
        in_specs=[
            pl.BlockSpec((rows, depth), lambda n: (0, 0)),
            pl.BlockSpec((rows, depth), lambda n: (0, 0)),
            pl.BlockSpec((depth, tile), lambda n: (0, n)),
            pl.BlockSpec((depth, tile), lambda n: (0, tiles + n)),
            pl.BlockSpec((depth, tile), lambda n: (0, 2 * tiles + n)),
        ],
        out_specs=[
            pl.BlockSpec((rows, tile), lambda n: (0, n)),
            pl.BlockSpec((rows, 2 * width), lambda n: (0, 0)),
        ],
        cost_estimate=pl.CostEstimate(
            flops=6 * rows * depth * width,
            bytes_accessed=4 * rows * depth + 6 * depth * width + 6 * rows * width,
            transcendentals=rows * width,
        ),
    )(h2, g_rows, wide, wide, wide)


def scores_of(q, k, seg_q, seg_k, row_base):
    s = lax.dot_general(q, k, (((1,), (1,)), ((), ())), preferred_element_type=F32) * (HD**-0.5)
    rows = lax.broadcasted_iota(jnp.int32, s.shape, 0) + row_base
    cols = lax.broadcasted_iota(jnp.int32, s.shape, 1)
    return jnp.where((seg_q == seg_k) & (rows >= cols), s, MASKED)


def softmax_of(s):
    peak = jnp.max(s, axis=-1, keepdims=True)
    e = jnp.exp(s - peak)
    return e * (1.0 / jnp.sum(e, axis=-1, keepdims=True))


def turn(values, cos, sin):
    return values * cos + pltpu.roll(values, HD // 2, 1) * sin


def attend_kernel(
    blocks, t_ref, q_ref, k_ref, v_ref, segc_ref, segr_ref, cos_ref, sin_ref,
    out_ref, saved_ref, kt, vt,
):
    size = q_ref.shape[0] // blocks
    width = saved_ref.shape[1] // 3
    head = pl.program_id(0) * HD
    t = t_ref[0]

    def rows(block):
        return pl.ds(pl.multiple_of((block ^ t) * size, size), size)

    def lanes(which):
        return pl.ds(pl.multiple_of(which * width + head, HD), HD)

    for b in range(blocks):
        lo, hi = b * size, (b + 1) * size
        cos, sin = cos_ref[lo:hi, :], sin_ref[lo:hi, :]
        q = turn(q_ref[rows(b), :], cos, sin).astype(BF16)
        k = turn(k_ref[rows(b), :], cos, sin).astype(BF16)
        v = v_ref[rows(b), :].astype(BF16)
        saved_ref[rows(b), lanes(0)] = q
        saved_ref[rows(b), lanes(1)] = k
        saved_ref[rows(b), lanes(2)] = v
        kt[lo:hi, :] = k
        vt[lo:hi, :] = v
        s = scores_of(q, kt[:hi, :], segc_ref[lo:hi, :], segr_ref[:, :hi], lo)
        p = softmax_of(s).astype(BF16)
        out_ref[rows(b), :] = jnp.dot(p, vt[:hi, :], preferred_element_type=F32).astype(BF16)


def attend_forward(t, pre, segc, segr, cos, sin):
    rows, width = pre.shape[0], pre.shape[1] // 3
    heads = width // HD
    blocks = lax.axis_size("tensor")
    table = pl.BlockSpec((rows, HD), lambda h, t: (0, 0))

    def kernel(*refs):
        attend_kernel(blocks, *refs)

    return pl.pallas_call(
        kernel,
        out_shape=[
            jax.ShapeDtypeStruct((rows, width), BF16),
            jax.ShapeDtypeStruct((rows, 3 * width), BF16),
        ],
        grid_spec=pltpu.PrefetchScalarGridSpec(
            num_scalar_prefetch=1,
            grid=(heads,),
            in_specs=[
                pl.BlockSpec((rows, HD), lambda h, t: (0, h)),
                pl.BlockSpec((rows, HD), lambda h, t: (0, heads + h)),
                pl.BlockSpec((rows, HD), lambda h, t: (0, 2 * heads + h)),
                pl.BlockSpec((rows, 1), lambda h, t: (0, 0)),
                pl.BlockSpec((1, rows), lambda h, t: (0, 0)),
                table,
                table,
            ],
            out_specs=[
                pl.BlockSpec((rows, HD), lambda h, t: (0, h)),
                pl.BlockSpec((rows, 3 * width), lambda h, t: (0, 0)),
            ],
            scratch_shapes=[pltpu.VMEM((rows, HD), BF16)] * 2,
        ),
        cost_estimate=pl.CostEstimate(
            flops=4 * rows * rows * width,
            bytes_accessed=20 * rows * width,
            transcendentals=rows * rows * heads,
        ),
    )(t, pre, pre, pre, segc, segr, cos, sin)


def unattend_kernel(
    blocks, t_ref, q_ref, k_ref, v_ref, g_ref, segc_ref, segr_ref, cos_ref, sin_ref,
    out_ref, kt, vt, dka, dva,
):
    size = q_ref.shape[0] // blocks
    width = out_ref.shape[1] // 3
    head = pl.program_id(0) * HD
    t = t_ref[0]

    def rows(block):
        return pl.ds(pl.multiple_of((block ^ t) * size, size), size)

    def lanes(which):
        return pl.ds(pl.multiple_of(which * width + head, HD), HD)

    def turn_back(grad, b):
        lo, hi = b * size, (b + 1) * size
        return grad * cos_ref[lo:hi, :] - pltpu.roll(grad, HD // 2, 1) * sin_ref[lo:hi, :]

    for b in range(blocks):
        kt[b * size : (b + 1) * size, :] = k_ref[rows(b), :]
        vt[b * size : (b + 1) * size, :] = v_ref[rows(b), :]
    for b in range(blocks - 1, -1, -1):
        n = (b + 1) * size
        q = q_ref[rows(b), :]
        g = g_ref[rows(b), :]
        s = scores_of(q, kt[:n, :], segc_ref[b * size : n, :], segr_ref[:, :n], b * size)
        p = softmax_of(s)
        dp = lax.dot_general(g, vt[:n, :], (((1,), (1,)), ((), ())), preferred_element_type=F32)
        pdp = p * dp
        delta = jnp.sum(pdp, axis=-1, keepdims=True)
        raw = ((pdp - p * delta) * (HD**-0.5)).astype(BF16)
        dq = jnp.dot(raw, kt[:n, :], preferred_element_type=F32)
        out_ref[rows(b), lanes(0)] = turn_back(dq, b).astype(BF16)
        dk = lax.dot_general(raw, q, (((0,), (0,)), ((), ())), preferred_element_type=F32)
        dv = lax.dot_general(
            p.astype(BF16), g, (((0,), (0,)), ((), ())), preferred_element_type=F32
        )
        if b == blocks - 1:
            dka[...] = dk
            dva[...] = dv
        else:
            dka[:n, :] += dk
            dva[:n, :] += dv
    for b in range(blocks):
        lo, hi = b * size, (b + 1) * size
        out_ref[rows(b), lanes(1)] = turn_back(dka[lo:hi, :], b).astype(BF16)
        out_ref[rows(b), lanes(2)] = dva[lo:hi, :].astype(BF16)


def attend_backward(t, saved, g, segc, segr, cos, sin):
    rows, width = g.shape
    heads = width // HD
    blocks = lax.axis_size("tensor")
    table = pl.BlockSpec((rows, HD), lambda h, t: (0, 0))

    def kernel(*refs):
        unattend_kernel(blocks, *refs)

    return pl.pallas_call(
        kernel,
        out_shape=jax.ShapeDtypeStruct((rows, 3 * width), BF16),
        grid_spec=pltpu.PrefetchScalarGridSpec(
            num_scalar_prefetch=1,
            grid=(heads,),
            in_specs=[
                pl.BlockSpec((rows, HD), lambda h, t: (0, h)),
                pl.BlockSpec((rows, HD), lambda h, t: (0, heads + h)),
                pl.BlockSpec((rows, HD), lambda h, t: (0, 2 * heads + h)),
                pl.BlockSpec((rows, HD), lambda h, t: (0, h)),
                pl.BlockSpec((rows, 1), lambda h, t: (0, 0)),
                pl.BlockSpec((1, rows), lambda h, t: (0, 0)),
                table,
                table,
            ],
            out_specs=pl.BlockSpec((rows, 3 * width), lambda h, t: (0, 0)),
            scratch_shapes=[pltpu.VMEM((rows, HD), BF16)] * 2 + [pltpu.VMEM((rows, HD), F32)] * 2,
        ),
        cost_estimate=pl.CostEstimate(
            flops=10 * rows * rows * width,
            bytes_accessed=14 * rows * width,
            transcendentals=rows * rows * heads,
        ),
    )(t, saved, saved, saved, g, segc, segr, cos, sin)


def per_device(
    tokens,
    lengths,
    query_weight,
    key_weight,
    value_weight,
    output_weight,
    gate_weight,
    up_weight,
    down_weight,
    cotangent,
):
    local = tokens.shape[0]
    group = lax.axis_size("tensor")
    t = lax.axis_index("tensor")
    slot_rows = local * group
    heads_width = query_weight.shape[1]
    hidden_width = gate_weight.shape[1]
    t_arg = t.astype(jnp.int32).reshape(1)

    half = hidden_width // 2

    mixed_own = pack_mixed(query_weight, key_weight, value_weight, output_weight)
    mixed_own, gate_weight, up_weight, down_weight = lax.optimization_barrier(
        (mixed_own, gate_weight, up_weight, down_weight)
    )
    mixed = gather_dp(mixed_own, 0)
    heads_full, out_full = mixed[:, : 3 * heads_width], mixed[:, 3 * heads_width :]
    wide = [
        gather_dp(
            jnp.concatenate(
                [w[:, a * half : (a + 1) * half] for w in (gate_weight, up_weight)]
                + [down_weight[a * half : (a + 1) * half].T],
                axis=1,
            ),
            0,
        )
        for a in range(2)
    ]

    segment, position, valid_all = slot_layout(lengths[0], slot_rows)
    valid = lax.dynamic_slice_in_dim(valid_all, t * local, local, 0).astype(F32)[:, None]
    cos, sin = rope_wide(position)
    segc, segr = segment[:, None], segment[None, :]

    residual = tokens.astype(F32)
    grad_out = cotangent.astype(F32) * valid
    normed_one, inverse_one = norm_forward(residual)
    h1, h1_own, h1_peer = gather_rows(normed_one.astype(BF16))
    g_rows, g_own, g_peer = gather_rows(after(grad_out.astype(BF16), h1))

    def rows_of(value, j):
        return value[j * local : (j + 1) * local]

    context, saved = attend_forward(t_arg, dot_plain(h1, heads_full), segc, segr, cos, sin)

    def attention_piece(j, earlier):
        rows = rows_of(context, j)
        return dot_last(rows if earlier is None else after(rows, earlier), out_full)

    middle = residual + scatter_rows(attention_piece)
    normed_two, inverse_two = norm_forward(middle)
    h2, h2_own, h2_peer = gather_rows(normed_two.astype(BF16))

    hidden_0, d_wide_0 = feed(h2, g_rows, wide[0])
    first_grad = pair_sum([(h2_own, h2_peer, d_wide_0), (g_own, g_peer, hidden_0)])
    first_sum = scatter_dp(first_grad)
    d_first = dot_last(d_wide_0, wide[0][:, : 2 * half])
    wide_1, first_grad, d_first = lax.optimization_barrier((wide[1], first_grad, d_first))
    hidden_1, d_wide_1 = feed(h2, g_rows, wide_1)

    pieces = []

    def feed_back_piece(j, earlier):
        rows = rows_of(d_wide_1, j)
        rows = rows if earlier is None else after(rows, earlier)
        pieces.append(rows_of(d_first, j) + dot_last(rows, wide_1[:, : 2 * half]))
        return pieces[-1]

    d_normed_two = scatter_rows(feed_back_piece)
    d_middle = grad_out + norm_backward(normed_two, inverse_two, d_normed_two)
    d_wide_1, hidden_1, _ = lax.optimization_barrier((d_wide_1, hidden_1, pieces[-1]))
    second_grad = pair_sum([(h2_own, h2_peer, d_wide_1), (g_own, g_peer, hidden_1)])
    (d_attention, d_attention_own, d_attention_peer), neighbours = gather_steps(d_middle.astype(BF16))
    second_sum = scatter_dp(after(second_grad, first_sum, *neighbours))

    d_context = dot_plain(d_attention, out_full).astype(BF16)
    d_pre = attend_backward(t_arg, saved, d_context, segc, segr, cos, sin)
    mixed_grad = pair_sum([(h1_own, h1_peer, d_pre), (d_attention_own, d_attention_peer, context)])
    mixed_sum = scatter_dp(after(mixed_grad, second_sum))

    def feed_piece(j, earlier):
        rows = after(rows_of(hidden_0, j), d_pre if earlier is None else earlier)
        return dot_last(rows, wide[0][:, 2 * half :]) + dot_last(
            rows_of(hidden_1, j), wide_1[:, 2 * half :]
        )

    feed_out = scatter_rows(feed_piece)
    output = (valid * (middle + feed_out)).astype(BF16)

    def heads_back_piece(j, earlier):
        rows = after(rows_of(d_pre, j), mixed_grad if earlier is None else earlier)
        return dot_last(rows, heads_full)

    d_normed_one = scatter_rows(heads_back_piece)
    input_grad = (d_middle + norm_backward(normed_one, inverse_one, d_normed_one)).astype(BF16)
    wide_sum = [after(first_sum, d_pre).astype(F32), after(second_sum, feed_out).astype(F32)]

    return (
        output,
        input_grad,
        *split_mixed(mixed_sum),
        jnp.concatenate([part[:, :half] for part in wide_sum], axis=1),
        jnp.concatenate([part[:, half : 2 * half] for part in wide_sum], axis=1),
        jnp.concatenate([part[:, 2 * half :].T for part in wide_sum], axis=0),
    )


def solution(mesh):
    return jax.shard_map(
        per_device,
        mesh=mesh,
        in_specs=(
            P(("dp", "tensor"), None),
            P("dp", None),
            P("dp", "tensor"),
            P("dp", "tensor"),
            P("dp", "tensor"),
            P("tensor", "dp"),
            P("dp", "tensor"),
            P("dp", "tensor"),
            P("tensor", "dp"),
            P(("dp", "tensor"), None),
        ),
        out_specs=(
            P(("dp", "tensor"), None),
            P(("dp", "tensor"), None),
            P("dp", "tensor"),
            P("dp", "tensor"),
            P("dp", "tensor"),
            P("tensor", "dp"),
            P("dp", "tensor"),
            P("dp", "tensor"),
            P("tensor", "dp"),
        ),
        check_vma=False,
    )
```

```python
import math

import jax
import jax.numpy as jnp
from jax import lax
from jax.experimental import pallas as pl
from jax.experimental.pallas import tpu as pltpu
from jax.sharding import PartitionSpec as P

HD = 128
EPSILON = 1e-05
ROPE_BASE = 10000.0
MASKED = -1e30
F32 = jnp.float32
BF16 = jnp.bfloat16


def norm_forward(rows):
    centre = jnp.mean(rows, axis=-1, keepdims=True)
    centered = rows - centre
    spread = jnp.mean(centered * centered, axis=-1, keepdims=True)
    inverse = lax.rsqrt(spread + EPSILON)
    return centered * inverse, inverse


def norm_backward(normed, inverse, grad):
    mean_grad = jnp.mean(grad, axis=-1, keepdims=True)
    mean_both = jnp.mean(grad * normed, axis=-1, keepdims=True)
    return (grad - mean_grad - normed * mean_both) * inverse


def slot_layout(lengths_row, row_total):
    ends = jnp.cumsum(lengths_row)
    places = jnp.arange(row_total, dtype=jnp.int32)
    segment = jnp.sum((places[:, None] >= ends[None, :]).astype(jnp.int32), axis=1)
    starts = jnp.concatenate([jnp.zeros((1,), jnp.int32), ends])
    picks = jnp.arange(starts.shape[0], dtype=jnp.int32)
    begins = jnp.sum(jnp.where(segment[:, None] == picks[None, :], starts[None, :], 0), axis=1)
    valid = (places < ends[-1]).astype(jnp.int32)
    return segment, places - begins, valid


def rope_wide(position):
    half = HD // 2
    steps = jnp.arange(half, dtype=F32)
    freqs = jnp.exp(steps * (-2.0 * math.log(ROPE_BASE) / HD))
    angles = position.astype(F32)[:, None] * freqs[None, :]
    cosine, sine = jnp.cos(angles), jnp.sin(angles)
    return (
        jnp.concatenate([cosine, cosine], axis=1),
        jnp.concatenate([-sine, sine], axis=1),
    )


def dot_plain(left, right):
    return jnp.dot(left, right, preferred_element_type=F32)


def dot_first(left, right):
    return lax.dot_general(left, right, (((0,), (0,)), ((), ())), preferred_element_type=F32)


def dot_last(left, right):
    return lax.dot_general(left, right, (((1,), (1,)), ((), ())), preferred_element_type=F32)


def after(value, *deps):
    return lax.optimization_barrier((value,) + deps)[0]


def gather_dp(own, axis):
    return lax.all_gather(own, "dp", axis=axis, tiled=True)


def core_swap(value):
    count = lax.axis_size("dp")
    return lax.ppermute(value, "dp", [(k, k ^ 1) for k in range(count)])


def pair_sum(terms):
    others = [core_swap(dot_first(peer, right).astype(BF16)) for own, peer, right in terms]
    sums = [
        (dot_first(own, right) + other.astype(F32)).astype(BF16)
        for (own, peer, right), other in zip(terms, others)
    ]
    return jnp.concatenate(sums, axis=1)


def scatter_dp(pairs):
    count = lax.axis_size("dp")
    groups = [list(range(core, count, 2)) for core in range(2)]
    return lax.psum_scatter(
        pairs, "dp", scatter_dimension=0, tiled=True, axis_index_groups=groups
    )


def pack_kernel(q_ref, k_ref, v_ref, o_ref, out_ref):
    width = q_ref.shape[1]
    for n, ref in enumerate((q_ref, k_ref, v_ref)):
        out_ref[:, n * width : (n + 1) * width] = ref[...]
    out_ref[:, 3 * width :] = o_ref[...].astype(F32).T.astype(BF16)


def pack_mixed(query, key, value, output):
    rows, width = query.shape
    tile = min(rows, 128)
    plain = pl.BlockSpec((tile, width), lambda n: (n, 0))
    return pl.pallas_call(
        pack_kernel,
        out_shape=jax.ShapeDtypeStruct((rows, 4 * width), BF16),
        grid=(rows // tile,),
        in_specs=[plain, plain, plain, pl.BlockSpec((width, tile), lambda n: (0, n))],
        out_specs=pl.BlockSpec((tile, 4 * width), lambda n: (n, 0)),
        cost_estimate=pl.CostEstimate(flops=0, bytes_accessed=16 * rows * width, transcendentals=0),
    )(query, key, value, output)


def split_kernel(in_ref, q_ref, k_ref, v_ref, o_ref):
    width = q_ref.shape[1]
    for n, ref in enumerate((q_ref, k_ref, v_ref)):
        ref[...] = in_ref[:, n * width : (n + 1) * width].astype(F32)
    o_ref[...] = in_ref[:, 3 * width :].astype(F32).T


def split_mixed(total):
    rows, width = total.shape[0], total.shape[1] // 4
    tile = min(rows, 128)
    plain = pl.BlockSpec((tile, width), lambda n: (n, 0))
    return pl.pallas_call(
        split_kernel,
        out_shape=[jax.ShapeDtypeStruct((rows, width), F32)] * 3
        + [jax.ShapeDtypeStruct((width, rows), F32)],
        grid=(rows // tile,),
        in_specs=[pl.BlockSpec((tile, 4 * width), lambda n: (n, 0))],
        out_specs=[plain, plain, plain, pl.BlockSpec((width, tile), lambda n: (0, n))],
        cost_estimate=pl.CostEstimate(flops=0, bytes_accessed=6 * total.size, transcendentals=0),
    )(total)


def flip(value, bits):
    return lax.ppermute(value, "tensor", [(k, k ^ bits) for k in range(lax.axis_size("tensor"))])


def join_kernel(core_ref, *refs):
    out, own, peer = refs[-3:]
    width = own.shape[1]
    mine = pl.multiple_of(core_ref[0] * width, width)
    other = pl.multiple_of((1 - core_ref[0]) * width, width)
    start = 0
    for ref in refs[:-3]:
        rows = slice(start, start + ref.shape[0])
        out[rows, :] = ref[...]
        own[rows, :] = ref[:, pl.ds(mine, width)]
        peer[rows, :] = ref[:, pl.ds(other, width)]
        start += ref.shape[0]


def join(pieces):
    rows = sum(piece.shape[0] for piece in pieces)
    width = pieces[0].shape[1]
    count = lax.axis_size("dp")
    tile = 2 * width // count
    core = (lax.axis_index("dp") % 2).astype(jnp.int32).reshape(1)
    half = pl.BlockSpec((rows, tile // 2), lambda n, c: (0, n))
    return pl.pallas_call(
        join_kernel,
        out_shape=[
            jax.ShapeDtypeStruct((rows, width), pieces[0].dtype),
            jax.ShapeDtypeStruct((rows, width // 2), pieces[0].dtype),
            jax.ShapeDtypeStruct((rows, width // 2), pieces[0].dtype),
        ],
        grid_spec=pltpu.PrefetchScalarGridSpec(
            num_scalar_prefetch=1,
            grid=(count // 2,),
            in_specs=[pl.BlockSpec((piece.shape[0], tile), lambda n, c: (0, n)) for piece in pieces],
            out_specs=[pl.BlockSpec((rows, tile), lambda n, c: (0, n)), half, half],
        ),
        cost_estimate=pl.CostEstimate(flops=0, bytes_accessed=6 * rows * width, transcendentals=0),
    )(core, *pieces)


def gather_rows(own):
    return gather_steps(own)[0]


def gather_steps(own):
    group = lax.axis_size("tensor")
    if group != 4:
        bits = 1
        while bits < group:
            own = jnp.concatenate([own, flip(own, bits)], axis=0)
            bits *= 2
        return join([own]), (own,)
    half = own.shape[0] // 2
    one = flip(own, 1)
    two = flip(own, 2)
    far_top = flip(one[:half], 2)
    far_low = flip(two[half:], 1)
    return join([own, one, two, far_top, far_low]), (one, two)


def scatter_rows(piece):
    group = lax.axis_size("tensor")
    if group != 4:
        parts = [piece(j, None).astype(BF16) for j in range(group)]
        while len(parts) > 1:
            bits = len(parts) // 2
            parts = [
                parts[j].astype(F32) + flip(parts[j + bits].astype(BF16), bits).astype(F32)
                for j in range(bits)
            ]
        return parts[0]
    far = piece(3, None).astype(BF16)
    half = far.shape[0] // 2
    top = flip(far[:half], 1)
    low = flip(far[half:], 2)
    one = piece(1, far).astype(BF16)
    one_top = flip(one[:half], 1)
    two = piece(2, one).astype(BF16)
    two_low = flip(two[half:], 2)
    one_low = flip((one[half:].astype(F32) + low.astype(F32)).astype(BF16), 1)
    two_top = flip((two[:half].astype(F32) + top.astype(F32)).astype(BF16), 2)
    own = lax.optimization_barrier(piece(0, two)).astype(F32)
    ones = jnp.concatenate([one_top, one_low], axis=0).astype(F32)
    twos = jnp.concatenate([two_top, two_low], axis=0).astype(F32)
    return own + ones + twos


def feed_kernel(h_ref, g_ref, gate_ref, up_ref, down_ref, hidden_ref, d_ref):
    tile = gate_ref.shape[1]
    lo = pl.program_id(0) * tile
    gate = jnp.dot(h_ref[...], gate_ref[...], preferred_element_type=F32)
    up = jnp.dot(h_ref[...], up_ref[...], preferred_element_type=F32)
    d_hidden = jnp.dot(g_ref[...], down_ref[...], preferred_element_type=F32)
    sg = jax.nn.sigmoid(gate)
    act = gate * sg
    hidden_ref[...] = (act * up).astype(BF16)
    d_gate = d_hidden * up * (sg + act * (1.0 - sg))
    d_ref[:, pl.ds(pl.multiple_of(lo, tile), tile)] = d_gate.astype(BF16)
    d_ref[:, pl.ds(pl.multiple_of(lo + d_ref.shape[1] // 2, tile), tile)] = (d_hidden * act).astype(BF16)


def feed(h2, g_rows, wide):
    rows, depth = h2.shape
    width = wide.shape[1] // 3
    tile = 256
    tiles = width // tile
    return pl.pallas_call(
        feed_kernel,
        out_shape=[
            jax.ShapeDtypeStruct((rows, width), BF16),
            jax.ShapeDtypeStruct((rows, 2 * width), BF16),
        ],
        grid=(tiles,),
        in_specs=[
            pl.BlockSpec((rows, depth), lambda n: (0, 0)),
            pl.BlockSpec((rows, depth), lambda n: (0, 0)),
            pl.BlockSpec((depth, tile), lambda n: (0, n)),
            pl.BlockSpec((depth, tile), lambda n: (0, tiles + n)),
            pl.BlockSpec((depth, tile), lambda n: (0, 2 * tiles + n)),
        ],
        out_specs=[
            pl.BlockSpec((rows, tile), lambda n: (0, n)),
            pl.BlockSpec((rows, 2 * width), lambda n: (0, 0)),
        ],
        cost_estimate=pl.CostEstimate(
            flops=6 * rows * depth * width,
            bytes_accessed=4 * rows * depth + 6 * depth * width + 6 * rows * width,
            transcendentals=rows * width,
        ),
    )(h2, g_rows, wide, wide, wide)


def scores_of(q, k, seg_q, seg_k, row_base):
    s = lax.dot_general(q, k, (((1,), (1,)), ((), ())), preferred_element_type=F32) * (HD**-0.5)
    rows = lax.broadcasted_iota(jnp.int32, s.shape, 0) + row_base
    cols = lax.broadcasted_iota(jnp.int32, s.shape, 1)
    return jnp.where((seg_q == seg_k) & (rows >= cols), s, MASKED)


def softmax_of(s):
    peak = jnp.max(s, axis=-1, keepdims=True)
    e = jnp.exp(s - peak)
    return e * (1.0 / jnp.sum(e, axis=-1, keepdims=True))


def turn(values, cos, sin):
    return values * cos + pltpu.roll(values, HD // 2, 1) * sin


def attend_kernel(
    blocks, t_ref, q_ref, k_ref, v_ref, segc_ref, segr_ref, cos_ref, sin_ref,
    out_ref, saved_ref, kt, vt,
):
    size = q_ref.shape[0] // blocks
    width = saved_ref.shape[1] // 3
    head = pl.program_id(0) * HD
    t = t_ref[0]

    def rows(block):
        return pl.ds(pl.multiple_of((block ^ t) * size, size), size)

    def lanes(which):
        return pl.ds(pl.multiple_of(which * width + head, HD), HD)

    for b in range(blocks):
        lo, hi = b * size, (b + 1) * size
        cos, sin = cos_ref[lo:hi, :], sin_ref[lo:hi, :]
        q = turn(q_ref[rows(b), :], cos, sin).astype(BF16)
        k = turn(k_ref[rows(b), :], cos, sin).astype(BF16)
        v = v_ref[rows(b), :].astype(BF16)
        saved_ref[rows(b), lanes(0)] = q
        saved_ref[rows(b), lanes(1)] = k
        saved_ref[rows(b), lanes(2)] = v
        kt[lo:hi, :] = k
        vt[lo:hi, :] = v
        s = scores_of(q, kt[:hi, :], segc_ref[lo:hi, :], segr_ref[:, :hi], lo)
        p = softmax_of(s).astype(BF16)
        out_ref[rows(b), :] = jnp.dot(p, vt[:hi, :], preferred_element_type=F32).astype(BF16)


def attend_forward(t, pre, segc, segr, cos, sin):
    rows, width = pre.shape[0], pre.shape[1] // 3
    heads = width // HD
    blocks = lax.axis_size("tensor")
    table = pl.BlockSpec((rows, HD), lambda h, t: (0, 0))

    def kernel(*refs):
        attend_kernel(blocks, *refs)

    return pl.pallas_call(
        kernel,
        out_shape=[
            jax.ShapeDtypeStruct((rows, width), BF16),
            jax.ShapeDtypeStruct((rows, 3 * width), BF16),
        ],
        grid_spec=pltpu.PrefetchScalarGridSpec(
            num_scalar_prefetch=1,
            grid=(heads,),
            in_specs=[
                pl.BlockSpec((rows, HD), lambda h, t: (0, h)),
                pl.BlockSpec((rows, HD), lambda h, t: (0, heads + h)),
                pl.BlockSpec((rows, HD), lambda h, t: (0, 2 * heads + h)),
                pl.BlockSpec((rows, 1), lambda h, t: (0, 0)),
                pl.BlockSpec((1, rows), lambda h, t: (0, 0)),
                table,
                table,
            ],
            out_specs=[
                pl.BlockSpec((rows, HD), lambda h, t: (0, h)),
                pl.BlockSpec((rows, 3 * width), lambda h, t: (0, 0)),
            ],
            scratch_shapes=[pltpu.VMEM((rows, HD), BF16)] * 2,
        ),
        cost_estimate=pl.CostEstimate(
            flops=4 * rows * rows * width,
            bytes_accessed=20 * rows * width,
            transcendentals=rows * rows * heads,
        ),
    )(t, pre, pre, pre, segc, segr, cos, sin)


def unattend_kernel(
    blocks, t_ref, q_ref, k_ref, v_ref, g_ref, segc_ref, segr_ref, cos_ref, sin_ref,
    out_ref, kt, vt, dka, dva,
):
    size = q_ref.shape[0] // blocks
    width = out_ref.shape[1] // 3
    head = pl.program_id(0) * HD
    t = t_ref[0]

    def rows(block):
        return pl.ds(pl.multiple_of((block ^ t) * size, size), size)

    def lanes(which):
        return pl.ds(pl.multiple_of(which * width + head, HD), HD)

    def turn_back(grad, b):
        lo, hi = b * size, (b + 1) * size
        return grad * cos_ref[lo:hi, :] - pltpu.roll(grad, HD // 2, 1) * sin_ref[lo:hi, :]

    for b in range(blocks):
        kt[b * size : (b + 1) * size, :] = k_ref[rows(b), :]
        vt[b * size : (b + 1) * size, :] = v_ref[rows(b), :]
    for b in range(blocks - 1, -1, -1):
        n = (b + 1) * size
        q = q_ref[rows(b), :]
        g = g_ref[rows(b), :]
        s = scores_of(q, kt[:n, :], segc_ref[b * size : n, :], segr_ref[:, :n], b * size)
        p = softmax_of(s)
        dp = lax.dot_general(g, vt[:n, :], (((1,), (1,)), ((), ())), preferred_element_type=F32)
        pdp = p * dp
        delta = jnp.sum(pdp, axis=-1, keepdims=True)
        raw = ((pdp - p * delta) * (HD**-0.5)).astype(BF16)
        dq = jnp.dot(raw, kt[:n, :], preferred_element_type=F32)
        out_ref[rows(b), lanes(0)] = turn_back(dq, b).astype(BF16)
        dk = lax.dot_general(raw, q, (((0,), (0,)), ((), ())), preferred_element_type=F32)
        dv = lax.dot_general(
            p.astype(BF16), g, (((0,), (0,)), ((), ())), preferred_element_type=F32
        )
        if b == blocks - 1:
            dka[...] = dk
            dva[...] = dv
        else:
            dka[:n, :] += dk
            dva[:n, :] += dv
    for b in range(blocks):
        lo, hi = b * size, (b + 1) * size
        out_ref[rows(b), lanes(1)] = turn_back(dka[lo:hi, :], b).astype(BF16)
        out_ref[rows(b), lanes(2)] = dva[lo:hi, :].astype(BF16)


def attend_backward(t, saved, g, segc, segr, cos, sin):
    rows, width = g.shape
    heads = width // HD
    blocks = lax.axis_size("tensor")
    table = pl.BlockSpec((rows, HD), lambda h, t: (0, 0))

    def kernel(*refs):
        unattend_kernel(blocks, *refs)

    return pl.pallas_call(
        kernel,
        out_shape=jax.ShapeDtypeStruct((rows, 3 * width), BF16),
        grid_spec=pltpu.PrefetchScalarGridSpec(
            num_scalar_prefetch=1,
            grid=(heads,),
            in_specs=[
                pl.BlockSpec((rows, HD), lambda h, t: (0, h)),
                pl.BlockSpec((rows, HD), lambda h, t: (0, heads + h)),
                pl.BlockSpec((rows, HD), lambda h, t: (0, 2 * heads + h)),
                pl.BlockSpec((rows, HD), lambda h, t: (0, h)),
                pl.BlockSpec((rows, 1), lambda h, t: (0, 0)),
                pl.BlockSpec((1, rows), lambda h, t: (0, 0)),
                table,
                table,
            ],
            out_specs=pl.BlockSpec((rows, 3 * width), lambda h, t: (0, 0)),
            scratch_shapes=[pltpu.VMEM((rows, HD), BF16)] * 2 + [pltpu.VMEM((rows, HD), F32)] * 2,
        ),
        cost_estimate=pl.CostEstimate(
            flops=10 * rows * rows * width,
            bytes_accessed=14 * rows * width,
            transcendentals=rows * rows * heads,
        ),
    )(t, saved, saved, saved, g, segc, segr, cos, sin)


def per_device(
    tokens,
    lengths,
    query_weight,
    key_weight,
    value_weight,
    output_weight,
    gate_weight,
    up_weight,
    down_weight,
    cotangent,
):
    local = tokens.shape[0]
    group = lax.axis_size("tensor")
    t = lax.axis_index("tensor")
    slot_rows = local * group
    heads_width = query_weight.shape[1]
    hidden_width = gate_weight.shape[1]
    t_arg = t.astype(jnp.int32).reshape(1)

    half = hidden_width // 2

    mixed_own = pack_mixed(query_weight, key_weight, value_weight, output_weight)
    mixed_own, gate_weight, up_weight, down_weight = lax.optimization_barrier(
        (mixed_own, gate_weight, up_weight, down_weight)
    )
    mixed = gather_dp(mixed_own, 0)
    heads_full, out_full = mixed[:, : 3 * heads_width], mixed[:, 3 * heads_width :]
    wide = [
        gather_dp(
            jnp.concatenate(
                [w[:, a * half : (a + 1) * half] for w in (gate_weight, up_weight)]
                + [down_weight[a * half : (a + 1) * half].T],
                axis=1,
            ),
            0,
        )
        for a in range(2)
    ]

    segment, position, valid_all = slot_layout(lengths[0], slot_rows)
    valid = lax.dynamic_slice_in_dim(valid_all, t * local, local, 0).astype(F32)[:, None]
    cos, sin = rope_wide(position)
    segc, segr = segment[:, None], segment[None, :]

    residual = tokens.astype(F32)
    grad_out = cotangent.astype(F32) * valid
    normed_one, inverse_one = norm_forward(residual)
    h1, h1_own, h1_peer = gather_rows(normed_one.astype(BF16))
    g_rows, g_own, g_peer = gather_rows(after(grad_out.astype(BF16), h1))

    def rows_of(value, j):
        return value[j * local : (j + 1) * local]

    context, saved = attend_forward(t_arg, dot_plain(h1, heads_full), segc, segr, cos, sin)

    def whole(value):
        return lambda j, earlier: rows_of(value, j)

    middle = residual + scatter_rows(whole(dot_last(context, out_full).astype(BF16)))
    normed_two, inverse_two = norm_forward(middle)
    h2, h2_own, h2_peer = gather_rows(normed_two.astype(BF16))

    hidden_0, d_wide_0 = feed(h2, g_rows, wide[0])
    first_grad = pair_sum([(h2_own, h2_peer, d_wide_0), (g_own, g_peer, hidden_0)])
    first_sum = scatter_dp(first_grad)
    d_first = dot_last(d_wide_0, wide[0][:, : 2 * half])
    wide_1, first_grad, d_first = lax.optimization_barrier((wide[1], first_grad, d_first))
    hidden_1, d_wide_1 = feed(h2, g_rows, wide_1)

    pieces = []

    def feed_back_piece(j, earlier):
        rows = rows_of(d_wide_1, j)
        rows = rows if earlier is None else after(rows, earlier)
        pieces.append(rows_of(d_first, j) + dot_last(rows, wide_1[:, : 2 * half]))
        return pieces[-1]

    d_normed_two = scatter_rows(feed_back_piece)
    d_middle = grad_out + norm_backward(normed_two, inverse_two, d_normed_two)
    d_wide_1, hidden_1, _ = lax.optimization_barrier((d_wide_1, hidden_1, pieces[-1]))
    second_grad = pair_sum([(h2_own, h2_peer, d_wide_1), (g_own, g_peer, hidden_1)])
    (d_attention, d_attention_own, d_attention_peer), neighbours = gather_steps(d_middle.astype(BF16))
    second_sum = scatter_dp(after(second_grad, first_sum, *neighbours))

    d_context = dot_plain(d_attention, out_full).astype(BF16)
    d_pre = attend_backward(t_arg, saved, d_context, segc, segr, cos, sin)
    mixed_grad = pair_sum([(h1_own, h1_peer, d_pre), (d_attention_own, d_attention_peer, context)])
    mixed_sum = scatter_dp(after(mixed_grad, second_sum))

    fed = dot_last(after(hidden_0, d_pre), wide[0][:, 2 * half :]) + dot_last(
        hidden_1, wide_1[:, 2 * half :]
    )
    feed_out = scatter_rows(whole(fed.astype(BF16)))
    output = (valid * (middle + feed_out)).astype(BF16)

    headed = dot_last(after(d_pre, mixed_grad), heads_full).astype(BF16)
    d_normed_one = scatter_rows(whole(headed))
    input_grad = (d_middle + norm_backward(normed_one, inverse_one, d_normed_one)).astype(BF16)
    wide_sum = [first_sum.astype(F32), second_sum.astype(F32)]

    return (
        output,
        input_grad,
        *split_mixed(mixed_sum),
        jnp.concatenate([part[:, :half] for part in wide_sum], axis=1),
        jnp.concatenate([part[:, half : 2 * half] for part in wide_sum], axis=1),
        jnp.concatenate([part[:, 2 * half :].T for part in wide_sum], axis=0),
    )


def solution(mesh):
    return jax.shard_map(
        per_device,
        mesh=mesh,
        in_specs=(
            P(("dp", "tensor"), None),
            P("dp", None),
            P("dp", "tensor"),
            P("dp", "tensor"),
            P("dp", "tensor"),
            P("tensor", "dp"),
            P("dp", "tensor"),
            P("dp", "tensor"),
            P("tensor", "dp"),
            P(("dp", "tensor"), None),
        ),
        out_specs=(
            P(("dp", "tensor"), None),
            P(("dp", "tensor"), None),
            P("dp", "tensor"),
            P("dp", "tensor"),
            P("dp", "tensor"),
            P("tensor", "dp"),
            P("dp", "tensor"),
            P("dp", "tensor"),
            P("tensor", "dp"),
        ),
        check_vma=False,
    )
```
